128 devices in a mesh: occ: 16 (over y, z_hi, core), vir: 8 (over x, z_lo).
Axes of the slice: x: 4, y: 4, z: 4 (z_hi: 2, z_lo: 2; z = z_hi * 2 + z_lo), core: 2. Of those that a mesh axis runs over, the one named last changes fastest.
Arguments:
- three_index: bfloat16 [2048, 128, 640], P(('occ', 'vir')), may hold values from -0.69921875 to 0.69921875
- virt_coeff: bfloat16 [640, 512], replicated, may hold values from -0.25 to 0.25
- metric_root: bfloat16 [2048, 2048], P(('occ', 'vir')), may hold values from -0.125 to 0.125
- owner_table: int32 [128], replicated, may hold values from 0 to 127, each once
- pair_order: int32 [4], replicated, may hold values from 0 to 15
- occ_energy: float32 [128], replicated, may hold values from -1.5 to -0.3
- vir_energy: float32 [512], replicated, may hold values from 0.1 to 2.5
Outputs:
- density: float32 [128, 512, 2048], P('occ', 'vir')
The draws below stay inside these ranges and needn't reach their ends.
Inputs may be any that keep to these rules, and one draw needn't show every extreme that they name: `owner_table`: each orbital once.
All inputs are finite; a program needn't handle non-finite values.
Results may differ from the reference program's by a relative error of at most 0.0045.
Values may be sent and summed in bfloat16 or wider, within the bound.
No kernel may reach another device: no remote copies, remote signals or barrier semaphores. Data moves between devices by JAX's collectives and lax.ppermute only.
A program may use at most 128 MiB of HBM per device.

```python
import jax
import jax.numpy as jnp
from jax import lax

NO = 128
NB = 640
NV = 512
NAUX = 2048
NSTEP = 4
N_OCC = 16
N_VIR = 8


def touch_ends(array, own_key, smallest, high):
    longest = array.shape.index(max(array.shape))
    spots = []
    for shift in (0, 1):
        where = [jax.random.randint(jax.random.fold_in(own_key, axis), (), 0, length) for axis, length in enumerate(array.shape)]
        where[longest] = (where[longest] + shift) % array.shape[longest]
        spots.append(tuple(where))
    return array.at[spots[0]].set(smallest).at[spots[1]].set(high)


def block_levels(own_key, shape, cuts, low, top_value):
    factor_of, own = 1.0, jax.random.fold_in(own_key, 6)
    for position, parts in cuts:
        heights = jnp.exp(jax.random.uniform(jax.random.fold_in(own, position), (parts,), jnp.float32, low / len(cuts), top_value / len(cuts)))
        factor_of = factor_of * jnp.repeat(heights, shape[position] // parts).reshape([-1 if axis == position else 1 for axis in range(len(shape))])
    return factor_of


def scatter_about(stream_key, shape, deviation, most, cuts=(), dtype=jnp.bfloat16):
    loudness = block_levels(stream_key, shape, cuts, -0.22, 0.18) if cuts else 1.0
    result = jax.random.normal(stream_key, shape, jnp.float32) * deviation * loudness
    return jnp.minimum(jnp.maximum(result, -most), most).astype(dtype)


def setup_inputs(seed: int = 0) -> dict:
    keys = jax.random.split(jax.random.key(seed), 8)
    return {
        "three_index": scatter_about(keys[0], (NAUX, NO, NB), 0.11, 0.69921875, ((0, 128),)),
        "virt_coeff": scatter_about(keys[1], (NB, NV), NB ** -0.5, 0.25),
        "metric_root": scatter_about(keys[2], (NAUX, NAUX), NAUX ** -0.5, 0.125, ((0, 128),)),
        "owner_table": jax.random.permutation(keys[3], NO).astype(jnp.int32),
        "pair_order": touch_ends(jax.random.randint(keys[4], (NSTEP,), 0, N_OCC), jax.random.fold_in(keys[4], 1), 0, N_OCC - 1).astype(jnp.int32),
        "occ_energy": jnp.clip(jax.random.uniform(keys[5], (NO,), jnp.float32, -1.5, -0.3), -1.5, -0.3),
        "vir_energy": jnp.clip(jax.random.uniform(keys[6], (NV,), jnp.float32, 0.1, 2.5), 0.1, 2.5),
    }


def reference(three_index, virt_coeff, metric_root, owner_table, pair_order, occ_energy, vir_energy):
    ordered = jnp.take(three_index, owner_table, axis=1)
    half = jnp.dot(ordered.reshape(NAUX * NO, NB), virt_coeff, preferred_element_type=jnp.float32)
    half = half.astype(jnp.bfloat16).reshape(NAUX, NO, NV)
    fitted = jnp.einsum("qp,pka->kaq", metric_root.astype(jnp.float32), half.astype(jnp.float32))
    fitted = fitted.astype(jnp.bfloat16)
    eps = occ_energy[owner_table]
    per_dev = NO // (N_OCC * N_VIR)
    block = NV // N_VIR
    density = jnp.zeros((NO, NV, NAUX), jnp.float32)
    for step in range(NSTEP):
        root = pair_order[step].astype(jnp.int32)
        pieces = []
        for vir_idx in range(N_VIR):
            start = ((root * N_VIR + vir_idx) * per_dev).astype(jnp.int32)
            partner = lax.dynamic_slice_in_dim(fitted, start, per_dev, 0).astype(jnp.float32)
            partner_eps = lax.dynamic_slice_in_dim(eps, start, per_dev, 0)
            own_rows = fitted[:, vir_idx * block:(vir_idx + 1) * block, :].astype(jnp.float32)
            block_eps = vir_energy[vir_idx * block:(vir_idx + 1) * block]
            pair = jnp.einsum("iaq,kbq->ikab", own_rows, partner)
            denom = (eps[:, None, None, None] + partner_eps[None, :, None, None]
                     - block_eps[None, None, :, None] - vir_energy[None, None, None, :])
            amp = (pair / denom).astype(jnp.bfloat16).astype(jnp.float32)
            pieces.append(jnp.einsum("ikab,kbq->iaq", amp, partner))
        density = density + jnp.concatenate(pieces, axis=1)
    return density
```

```python
import numpy as np
import jax
import jax.numpy as jnp
from jax import lax
from jax.experimental import pallas as pl
from jax.experimental.pallas import tpu as pltpu
from jax.sharding import PartitionSpec as P


AXES = ("occ", "vir")
SIZE = {"x": 4, "y": 4, "z": 4}
ORDER = (("z", "x", "y"), ("y", "z", "x"))


def line(p):
    return ((p["y"] * 2 + p["z"] // 2) * 2 + p["c"]) * 8 + p["x"] * 2 + p["z"] % 2


def places():
    return [
        dict(x=x, y=y, z=z, c=c)
        for x in range(4)
        for y in range(4)
        for z in range(4)
        for c in range(2)
    ]


def moved(p, dim, by):
    q = dict(p)
    q[dim] = (q[dim] + by) % SIZE[dim]
    return q


def shifted(value, dims, by):
    pairs = [(line(p), line(moved(p, dims[p["c"]], by))) for p in places()]
    return lax.ppermute(value, AXES, pairs)


def swapped(value):
    pairs = [(line(p), line(dict(p, c=1 - p["c"]))) for p in places()]
    return lax.ppermute(value, AXES, pairs)


def metric_table():
    table = np.zeros((128, 8, 16), np.int32)
    for p in places():
        for buf in range(8):
            core = p["c"] if buf < 4 else 1 - p["c"]
            first, second, third = ORDER[core]
            for k2 in range(4):
                for k1 in range(4):
                    q = dict(p, c=core)
                    for dim, by in ((third, buf % 4), (second, k2), (first, k1)):
                        q = moved(q, dim, -by)
                    table[line(p), buf, k2 * 4 + k1] = line(q)
    return table


def partner_table():
    chunk = np.zeros((128, 64), np.int32)
    step = np.zeros((64,), np.int32)
    for p in places():
        at = 0
        for core in (p["c"], 1 - p["c"]):
            for ky in range(4):
                for kz in range(2):
                    for s in (0, 1):
                        q = moved(moved(dict(p, c=core), "y", -ky), "z", 2 * kz)
                        chunk[line(p), at] = line(q) // 8
                        step[at] = s
                        at += 1
            for kz in range(2):
                for ky in range(4):
                    for s in (2, 3):
                        q = moved(moved(dict(p, c=core), "y", -ky), "z", 2 * kz)
                        chunk[line(p), at] = line(q) // 8
                        step[at] = s
                        at += 1
    return chunk, step


def gathered_metric(rows):
    for stage in (0, 1):
        dims = (ORDER[0][stage], ORDER[1][stage])
        rows = jnp.concatenate([rows] + [shifted(rows, dims, by) for by in (1, 2, 3)], axis=0)
    dims = (ORDER[0][2], ORDER[1][2])
    mine = [rows] + [shifted(rows, dims, by) for by in (1, 3, 2)]
    mine = [mine[0], mine[1], mine[3], mine[2]]
    return mine + [swapped(part) for part in mine]


def arrange_kernel(own_ref, part_ref, out_ref):
    group = pl.program_id(0)
    lane = lax.broadcasted_iota(jnp.int32, (16, 128), 1)
    low = lane < 64
    back = (4 - lax.rem(group, 4)) * 32
    for pairs in range(4):
        at = slice(pairs * 128, pairs * 128 + 128)
        for j in range(4):
            even = own_ref[2 * j, :, at].astype(jnp.float32)
            odd = own_ref[2 * j + 1, :, at].astype(jnp.float32)
            to = slice(j * 128, j * 128 + 128)
            first = jnp.where(low, even, pltpu.roll(odd, 64, 1))
            second = jnp.where(low, pltpu.roll(even, 64, 1), odd)
            out_ref[2 * pairs, :, to] = first.astype(out_ref.dtype)
            out_ref[2 * pairs + 1, :, to] = second.astype(out_ref.dtype)
    for v in range(8):
        total = jnp.zeros((16, 128), jnp.float32)
        for s in range(4):
            tile = part_ref[s * 8 + v].astype(jnp.float32)
            tile = pltpu.roll(tile, lax.rem(back + 32 * s, 128), 1)
            total = jnp.where(lane // 32 == s, tile, total)
        out_ref[v, :, 512:640] = total.astype(out_ref.dtype)


def arrange(chosen):
    return pl.pallas_call(
        arrange_kernel,
        grid=(16,),
        in_specs=[
            pl.BlockSpec((8, 16, 512), lambda o: (o, 0, 0)),
            pl.BlockSpec((32, 16, 128), lambda o: (4, 0, o // 4)),
        ],
        out_specs=pl.BlockSpec((8, 16, 640), lambda o: (o, 0, 0)),
        out_shape=jax.ShapeDtypeStruct((128, 16, 640), jnp.bfloat16),
        name="arrange",
    )(chosen, chosen)


def place_kernel(table_ref, *refs):
    parts, out_ref, sems = refs[:8], refs[8], refs[9]
    for buf in range(8):

        def start(j, carry, buf=buf):
            row = pl.multiple_of(table_ref[buf * 16 + j] * 16, 16)
            pltpu.make_async_copy(
                parts[buf].at[pl.ds(pl.multiple_of(j * 16, 16), 16)],
                out_ref.at[pl.ds(row, 16)],
                sems.at[buf],
            ).start()
            return carry

        lax.fori_loop(0, 16, start, 0)
    for buf in range(8):
        pltpu.make_async_copy(parts[buf], out_ref.at[pl.ds(0, 256)], sems.at[buf]).wait()


def place(table, parts):
    return pl.pallas_call(
        place_kernel,
        in_specs=[pl.BlockSpec(memory_space=pltpu.SMEM)] + [pl.BlockSpec(memory_space=pl.ANY)] * 8,
        out_specs=pl.BlockSpec(memory_space=pl.ANY),
        out_shape=jax.ShapeDtypeStruct((2048, 2048), jnp.bfloat16),
        scratch_shapes=[pltpu.SemaphoreType.DMA((8,))],
        name="place",
    )(table, *parts)


def pair_kernel(own_ref, row_ref, col_ref, *refs):
    parts, out_ref, buf, sems = refs[:12], refs[12], refs[13], refs[14]
    copies, at = [], 0
    for i, part in enumerate(parts):
        rows = part.shape[0]
        copies.append((at, pltpu.make_async_copy(part, buf.at[pl.ds(at, rows)], sems.at[i])))
        at += rows
    for _, copy in copies:
        copy.start()
    row = row_ref[:, :1]
    for block in range(8):
        for start, copy in copies:
            if block * 256 <= start < block * 256 + 256:
                copy.wait()
        part = buf[block * 256:block * 256 + 256, :]
        pair = lax.dot_general(
            own_ref[...], part, (((1,), (1,)), ((), ())), preferred_element_type=jnp.float32
        )
        amp = (pair / (row + col_ref[block:block + 1, :])).astype(jnp.bfloat16)
        term = jnp.dot(amp, part, preferred_element_type=jnp.float32)
        if block == 0:
            out_ref[...] = term
        else:
            out_ref[...] += term


def paired(own, row, col, parts):
    vmem = pl.BlockSpec(memory_space=pltpu.VMEM)
    return pl.pallas_call(
        pair_kernel,
        in_specs=[vmem] * 3 + [pl.BlockSpec(memory_space=pl.ANY)] * 12,
        out_specs=vmem,
        out_shape=jax.ShapeDtypeStruct((512, 2048), jnp.float32),
        scratch_shapes=[pltpu.VMEM((2048, 2048), jnp.bfloat16), pltpu.SemaphoreType.DMA((12,))],
        name="pair",
    )(own, row, col, *parts)


def local(three_index, virt_coeff, metric_root, owner_table, pair_order, occ_energy, vir_energy):
    occ_idx = lax.axis_index("occ")
    vir_idx = lax.axis_index("vir")
    me = occ_idx * 8 + vir_idx

    metric_parts = gathered_metric(metric_root)

    half = jnp.dot(
        three_index.reshape(16 * 128, 640), virt_coeff, preferred_element_type=jnp.float32
    )
    half = half.astype(jnp.bfloat16).reshape(16, 128, 512).transpose(1, 0, 2)
    partners = [lax.dynamic_slice_in_dim(owner_table, pair_order[s] * 8, 8, 0) for s in range(4)]
    index = jnp.concatenate([owner_table] + partners)
    chosen = half.at[index].get(mode="promise_in_bounds")
    sent = arrange(chosen)
    owned = lax.all_to_all(sent, AXES, split_axis=0, concat_axis=0, tiled=True).reshape(2048, 640)

    table = lax.dynamic_slice_in_dim(jnp.asarray(metric_table()), me, 1, 0).reshape(128)
    metric = place(table, metric_parts)

    def fit(rows):
        return lax.dot_general(
            rows, metric, (((0,), (1,)), ((), ())), preferred_element_type=jnp.float32
        ).astype(jnp.bfloat16)

    mine = fit(owned[:, 512:])
    own = fit(owned[:, :512])

    ydim, zdim = ("y", "y"), ("z", "z")
    early, late = mine[:64], mine[64:]
    early = jnp.concatenate([early, shifted(early, zdim, 2)], axis=0)
    late = jnp.concatenate([late] + [shifted(late, ydim, by) for by in (1, 2, 3)], axis=0)
    parts = [early] + [shifted(early, ydim, by) for by in (1, 2, 3)]
    parts += [late, shifted(late, zdim, 2)]
    parts += [swapped(part) for part in parts]

    one_hot = (owner_table[:, None] == jnp.arange(128, dtype=jnp.int32)[None, :]).astype(jnp.float32)
    eps = jnp.dot(one_hot, occ_energy, precision=lax.Precision.HIGHEST)
    own_eps = lax.dynamic_slice_in_dim(eps, occ_idx * 8, 8, 0)
    block_eps = lax.dynamic_slice_in_dim(vir_energy, vir_idx * 64, 64, 0)
    row = (own_eps[:, None] - block_eps[None, :]).reshape(512, 1)
    row = jnp.broadcast_to(row, (512, 128))
    chunks, steps = partner_table()
    chunk = lax.dynamic_slice_in_dim(jnp.asarray(chunks), me, 1, 0).reshape(64)
    pick = (chunk[:, None] == jnp.arange(16, dtype=jnp.int32)[None, :]).astype(jnp.float32)
    vir_rows = jnp.dot(pick, vir_energy.reshape(16, 32), precision=lax.Precision.HIGHEST)
    partner_eps = jnp.concatenate(
        [lax.dynamic_slice_in_dim(eps, pair_order[s] * 8 + vir_idx, 1, 0) for s in range(4)]
    )
    which = jnp.asarray((steps[:, None] == np.arange(4)[None, :]).astype(np.float32))
    eps_rows = jnp.dot(which, partner_eps[:, None], precision=lax.Precision.HIGHEST)
    col = (eps_rows - vir_rows).reshape(8, 256)

    density = paired(own, row, col, parts)
    return density.reshape(8, 64, 2048)


def solution(mesh):
    placed = (P(AXES, None, None), P(), P(AXES, None), P(), P(), P(), P())
    return jax.shard_map(
        local, mesh=mesh, in_specs=placed, out_specs=P("occ", "vir", None), check_vma=False
    )
```

```python
import numpy as np
import jax
import jax.numpy as jnp
from jax import lax
from jax.experimental import pallas as pl
from jax.experimental.pallas import tpu as pltpu
from jax.sharding import PartitionSpec as P


AXES = ("occ", "vir")
SIZE = {"x": 4, "y": 4, "z": 4}
ORDER = (("z", "x", "y"), ("y", "z", "x"))


def line(p):
    return ((p["y"] * 2 + p["z"] // 2) * 2 + p["c"]) * 8 + p["x"] * 2 + p["z"] % 2


def places():
    return [
        dict(x=x, y=y, z=z, c=c)
        for x in range(4)
        for y in range(4)
        for z in range(4)
        for c in range(2)
    ]


def moved(p, dim, by):
    q = dict(p)
    q[dim] = (q[dim] + by) % SIZE[dim]
    return q


def shifted(value, dims, by):
    pairs = [(line(p), line(moved(p, dims[p["c"]], by))) for p in places()]
    return lax.ppermute(value, AXES, pairs)


def swapped(value):
    pairs = [(line(p), line(dict(p, c=1 - p["c"]))) for p in places()]
    return lax.ppermute(value, AXES, pairs)


def metric_table():
    table = np.zeros((128, 8, 16), np.int32)
    for p in places():
        for buf in range(8):
            core = p["c"] if buf < 4 else 1 - p["c"]
            first, second, third = ORDER[core]
            for k2 in range(4):
                for k1 in range(4):
                    q = dict(p, c=core)
                    for dim, by in ((third, buf % 4), (second, k2), (first, k1)):
                        q = moved(q, dim, -by)
                    table[line(p), buf, k2 * 4 + k1] = line(q)
    return table


def partner_table():
    chunk = np.zeros((128, 64), np.int32)
    step = np.zeros((64,), np.int32)
    for p in places():
        at = 0
        for core in (p["c"], 1 - p["c"]):
            for ky in range(4):
                for kz in range(2):
                    for s in (0, 1):
                        q = moved(moved(dict(p, c=core), "y", -ky), "z", 2 * kz)
                        chunk[line(p), at] = line(q) // 8
                        step[at] = s
                        at += 1
            for kz in range(2):
                for ky in range(4):
                    for s in (2, 3):
                        q = moved(moved(dict(p, c=core), "y", -ky), "z", 2 * kz)
                        chunk[line(p), at] = line(q) // 8
                        step[at] = s
                        at += 1
    return chunk, step


def gathered_metric(rows):
    for stage in (0, 1):
        dims = (ORDER[0][stage], ORDER[1][stage])
        rows = jnp.concatenate([rows] + [shifted(rows, dims, by) for by in (1, 2, 3)], axis=0)
    dims = (ORDER[0][2], ORDER[1][2])
    mine = [rows] + [shifted(rows, dims, by) for by in (1, 3, 2)]
    mine = [mine[0], mine[1], mine[3], mine[2]]
    return mine + [swapped(part) for part in mine]


def half_kernel(pick_ref, ints_ref, coeff_ref, out_ref, scratch):
    def select(p, carry):
        half = jnp.dot(ints_ref[p], coeff_ref[...], preferred_element_type=jnp.float32)
        rows = jnp.dot(
            pick_ref[...], half.astype(jnp.bfloat16), preferred_element_type=jnp.float32
        )
        for t in range(4):
            scratch.at[t][pl.ds(p, 160, stride=16), :] = rows[:, t * 128:t * 128 + 128]
        return carry

    lax.fori_loop(0, 16, select, 0)
    lane = lax.broadcasted_iota(jnp.int32, (16, 128), 1)
    low = lane < 64

    def emit(group, carry):
        first_row = pl.multiple_of(group * 128, 128)
        to = pl.multiple_of(group * 8, 8)
        for t in range(4):
            for j in range(4):
                even = scratch[t, pl.ds(first_row + 32 * j, 16), :]
                odd = scratch[t, pl.ds(first_row + 32 * j + 16, 16), :]
                first = jnp.where(low, even, pltpu.roll(odd, 64, 1))
                second = jnp.where(low, pltpu.roll(even, 64, 1), odd)
                at = slice(j * 128, j * 128 + 128)
                out_ref[to + 2 * t, :, at] = first.astype(out_ref.dtype)
                out_ref[to + 2 * t + 1, :, at] = second.astype(out_ref.dtype)
        return carry

    lax.fori_loop(0, 16, emit, 0)

    def emit_partner(v, carry):
        for t in range(4):
            tiles = [
                scratch[t, pl.ds(pl.multiple_of((128 + s * 8 + v) * 16, 16), 16), :]
                for s in range(4)
            ]
            for g in range(4):
                total = jnp.zeros((16, 128), jnp.float32)
                for s in range(4):
                    by = (s - g) * 32 % 128
                    tile = pltpu.roll(tiles[s], by, 1) if by else tiles[s]
                    total = jnp.where(lane // 32 == s, tile, total)
                out_ref[(t * 4 + g) * 8 + v, :, 512:640] = total.astype(out_ref.dtype)
        return carry

    lax.fori_loop(0, 8, emit_partner, 0)


def transformed(pick, three_index, virt_coeff):
    vmem = pl.BlockSpec(memory_space=pltpu.VMEM)
    return pl.pallas_call(
        half_kernel,
        in_specs=[vmem] * 3,
        out_specs=vmem,
        out_shape=jax.ShapeDtypeStruct((128, 16, 640), jnp.bfloat16),
        scratch_shapes=[pltpu.VMEM((4, 160 * 16, 128), jnp.float32)],
        name="half",
    )(pick, three_index, virt_coeff)


def fit_kernel(table_ref, rows_ref, *refs, first, width, outs):
    parts, out_refs = refs[:8], refs[8:8 + outs]
    rows, metric, sems, row_sem = refs[8 + outs:]
    take = pltpu.make_async_copy(rows_ref.at[:, pl.ds(first, width)], rows, row_sem)
    take.start()
    for buf in range(8):

        def start(j, carry, buf=buf):
            row = pl.multiple_of(table_ref[buf * 16 + j] * 16, 16)
            pltpu.make_async_copy(
                parts[buf].at[pl.ds(pl.multiple_of(j * 16, 16), 16)],
                metric.at[pl.ds(row, 16)],
                sems.at[buf],
            ).start()
            return carry

        lax.fori_loop(0, 16, start, 0)
    take.wait()
    left = rows[...].T
    for buf in range(8):
        pltpu.make_async_copy(parts[buf], metric.at[pl.ds(0, 256)], sems.at[buf]).wait()
    each = width // outs
    for block in range(4):
        at = slice(block * 512, block * 512 + 512)
        fitted = lax.dot_general(
            left, metric[at, :], (((1,), (1,)), ((), ())), preferred_element_type=jnp.float32
        ).astype(jnp.bfloat16)
        for i in range(outs):
            out_refs[i][:, at] = fitted[i * each:i * each + each]


def fit(table, owned, parts, first, width, outs):
    vmem = pl.BlockSpec(memory_space=pltpu.VMEM)
    shape = jax.ShapeDtypeStruct((width // outs, 2048), jnp.bfloat16)

    def body(*refs):
        fit_kernel(*refs, first=first, width=width, outs=outs)

    return pl.pallas_call(
        body,
        in_specs=[pl.BlockSpec(memory_space=pltpu.SMEM)] + [pl.BlockSpec(memory_space=pl.ANY)] * 9,
        out_specs=[vmem] * outs,
        out_shape=[shape] * outs,
        scratch_shapes=[
            pltpu.VMEM((2048, width), jnp.bfloat16),
            pltpu.VMEM((2048, 2048), jnp.bfloat16),
            pltpu.SemaphoreType.DMA((8,)),
            pltpu.SemaphoreType.DMA,
        ],
        name="fit_own" if outs == 1 else "fit_partner",
    )(table, owned, *parts)


def pair_kernel(own_ref, row_ref, col_ref, *refs):
    parts, out_ref, buf, sems = refs[:12], refs[12], refs[13], refs[14]
    copies, at = [], 0
    for i, part in enumerate(parts):
        rows = part.shape[0]
        copies.append((at, pltpu.make_async_copy(part, buf.at[pl.ds(at, rows)], sems.at[i])))
        at += rows
    for _, copy in copies:
        copy.start()
    row = row_ref[:, :1]
    for block in range(4):
        for start, copy in copies:
            if block * 512 <= start < block * 512 + 512:
                copy.wait()
        part = buf[block * 512:block * 512 + 512, :]
        pair = lax.dot_general(
            own_ref[...], part, (((1,), (1,)), ((), ())), preferred_element_type=jnp.float32
        )
        amp = (pair / (row + col_ref[block:block + 1, :])).astype(jnp.bfloat16)
        term = jnp.dot(amp, part, preferred_element_type=jnp.float32)
        if block == 0:
            out_ref[...] = term
        else:
            out_ref[...] += term


def paired(own, row, col, parts):
    vmem = pl.BlockSpec(memory_space=pltpu.VMEM)
    return pl.pallas_call(
        pair_kernel,
        in_specs=[vmem] * 3 + [pl.BlockSpec(memory_space=pl.ANY)] * 12,
        out_specs=vmem,
        out_shape=jax.ShapeDtypeStruct((512, 2048), jnp.float32),
        scratch_shapes=[pltpu.VMEM((2048, 2048), jnp.bfloat16), pltpu.SemaphoreType.DMA((12,))],
        name="pair",
    )(own, row, col, *parts)


def local(three_index, virt_coeff, metric_root, owner_table, pair_order, occ_energy, vir_energy):
    occ_idx = lax.axis_index("occ")
    vir_idx = lax.axis_index("vir")
    me = occ_idx * 8 + vir_idx

    metric_parts = gathered_metric(metric_root)

    partners = [lax.dynamic_slice_in_dim(owner_table, pair_order[s] * 8, 8, 0) for s in range(4)]
    index = jnp.concatenate([owner_table] + partners)
    pick = (index[:, None] == jnp.arange(128, dtype=jnp.int32)[None, :]).astype(jnp.bfloat16)
    sent = transformed(pick, three_index, virt_coeff)
    owned = lax.all_to_all(sent, AXES, split_axis=0, concat_axis=0, tiled=True).reshape(2048, 640)

    table = lax.dynamic_slice_in_dim(jnp.asarray(metric_table()), me, 1, 0).reshape(128)
    early, late = fit(table, owned, metric_parts, 512, 128, 2)
    (own,) = fit(table, owned, metric_parts, 0, 512, 1)

    ydim, zdim = ("y", "y"), ("z", "z")
    early = jnp.concatenate([early, shifted(early, zdim, 2)], axis=0)
    late = jnp.concatenate([late] + [shifted(late, ydim, by) for by in (1, 2, 3)], axis=0)
    parts = [early] + [shifted(early, ydim, by) for by in (1, 2, 3)]
    parts += [late, shifted(late, zdim, 2)]
    parts += [swapped(part) for part in parts]

    one_hot = (owner_table[:, None] == jnp.arange(128, dtype=jnp.int32)[None, :]).astype(jnp.float32)
    eps = jnp.dot(one_hot, occ_energy, precision=lax.Precision.HIGHEST)
    own_eps = lax.dynamic_slice_in_dim(eps, occ_idx * 8, 8, 0)
    block_eps = lax.dynamic_slice_in_dim(vir_energy, vir_idx * 64, 64, 0)
    row = (own_eps[:, None] - block_eps[None, :]).reshape(512, 1)
    row = jnp.broadcast_to(row, (512, 128))
    chunks, steps = partner_table()
    chunk = lax.dynamic_slice_in_dim(jnp.asarray(chunks), me, 1, 0).reshape(64)
    pick = (chunk[:, None] == jnp.arange(16, dtype=jnp.int32)[None, :]).astype(jnp.float32)
    vir_rows = jnp.dot(pick, vir_energy.reshape(16, 32), precision=lax.Precision.HIGHEST)
    partner_eps = jnp.concatenate(
        [lax.dynamic_slice_in_dim(eps, pair_order[s] * 8 + vir_idx, 1, 0) for s in range(4)]
    )
    which = jnp.asarray((steps[:, None] == np.arange(4)[None, :]).astype(np.float32))
    eps_rows = jnp.dot(which, partner_eps[:, None], precision=lax.Precision.HIGHEST)
    col = (eps_rows - vir_rows).reshape(4, 512)

    density = paired(own, row, col, parts)
    return density.reshape(8, 64, 2048)


def solution(mesh):
    placed = (P(AXES, None, None), P(), P(AXES, None), P(), P(), P(), P())
    return jax.shard_map(
        local, mesh=mesh, in_specs=placed, out_specs=P("occ", "vir", None), check_vma=False
    )
```

```python
import numpy as np
import jax
import jax.numpy as jnp
from jax import lax
from jax.experimental import pallas as pl
from jax.experimental.pallas import tpu as pltpu
from jax.sharding import PartitionSpec as P


AXES = ("occ", "vir")
SIZE = {"x": 4, "y": 4, "z": 4}
ORDER = (("z", "x", "y"), ("y", "z", "x"))


def line(p):
    return ((p["y"] * 2 + p["z"] // 2) * 2 + p["c"]) * 8 + p["x"] * 2 + p["z"] % 2


def places():
    return [
        dict(x=x, y=y, z=z, c=c)
        for x in range(4)
        for y in range(4)
        for z in range(4)
        for c in range(2)
    ]


def moved(p, dim, by):
    q = dict(p)
    q[dim] = (q[dim] + by) % SIZE[dim]
    return q


def shifted(value, dims, by):
    pairs = [(line(p), line(moved(p, dims[p["c"]], by))) for p in places()]
    return lax.ppermute(value, AXES, pairs)


def swapped(value):
    pairs = [(line(p), line(dict(p, c=1 - p["c"]))) for p in places()]
    return lax.ppermute(value, AXES, pairs)


def metric_table():
    table = np.zeros((128, 8, 16), np.int32)
    for p in places():
        for buf in range(8):
            core = p["c"] if buf < 4 else 1 - p["c"]
            first, second, third = ORDER[core]
            for k2 in range(4):
                for k1 in range(4):
                    q = dict(p, c=core)
                    for dim, by in ((third, buf % 4), (second, k2), (first, k1)):
                        q = moved(q, dim, -by)
                    table[line(p), buf, k2 * 4 + k1] = line(q)
    return table


FIRST = ((("l", 0, 0), ("e", 0, 0), ("e", 0, 1)), (("l", 0, 1),))
SECOND = (
    (("e", 1, 0), ("e", 3, 0), ("e", 1, 1), ("e", 3, 1)),
    (("e", 2, 0), ("e", 2, 1), ("l", 1, 0)),
    (("l", 1, 1),),
)


def partner_table():
    chunk = np.zeros((128, 64), np.int32)
    step = np.zeros((64,), np.int32)
    for p in places():
        at = 0
        for kind, by, other in [key for group in FIRST + SECOND for key in group]:
            core = 1 - p["c"] if other else p["c"]
            if kind == "e":
                inner = [(by, kz, s) for kz in range(2) for s in (0, 1)]
            else:
                inner = [(ky, by, s) for ky in range(4) for s in (2, 3)]
            for ky, kz, s in inner:
                q = moved(moved(dict(p, c=core), "y", -ky), "z", 2 * kz)
                chunk[line(p), at] = line(q) // 8
                step[at] = s
                at += 1
    return chunk, step


def gathered_metric(rows):
    for stage in (0, 1):
        dims = (ORDER[0][stage], ORDER[1][stage])
        got = [shifted(rows, dims, by) for by in (1, 2, 3)]
        rows = jnp.concatenate([rows] + got, axis=0)
    dims = (ORDER[0][2], ORDER[1][2])
    mine = [rows] + [shifted(rows, dims, by) for by in (1, 2, 3)]
    return mine + [swapped(part) for part in mine]


def half_kernel(order_ref, owner_ref, ints_ref, coeff_ref, out_ref, scratch, pick_ref):
    owners = jnp.broadcast_to(owner_ref[...].astype(jnp.float32), (128, 128)).T
    orbital = lax.broadcasted_iota(jnp.int32, (128, 128), 1).astype(jnp.float32)
    pick_ref[0:128, :] = jnp.where(owners == orbital, 1.0, 0.0)
    for s in range(4):
        first = pl.multiple_of(order_ref[s] * 8, 8)
        pick_ref[128 + 8 * s:136 + 8 * s, :] = pick_ref[pl.ds(first, 8), :]
    pick = pick_ref[...].astype(jnp.bfloat16)

    def select(c, carry):
        half = jnp.dot(
            ints_ref[pl.ds(c * 4, 4)].reshape(512, 640),
            coeff_ref[...],
            preferred_element_type=jnp.float32,
        ).astype(jnp.bfloat16)
        for i in range(4):
            rows = jnp.dot(
                pick, half[i * 128:i * 128 + 128], preferred_element_type=jnp.float32
            )
            for t in range(4):
                at = pl.ds(c * 4 + i, 160, stride=16)
                scratch.at[t][at, :] = rows[:, t * 128:t * 128 + 128]
        return carry

    lax.fori_loop(0, 4, select, 0)
    lane = lax.broadcasted_iota(jnp.int32, (16, 128), 1)
    low = lane < 64

    def emit(group, carry):
        first_row = pl.multiple_of(group * 128, 128)
        to = pl.multiple_of(group * 8, 8)
        for t in range(4):
            for j in range(4):
                even = scratch[t, pl.ds(first_row + 32 * j, 16), :]
                odd = scratch[t, pl.ds(first_row + 32 * j + 16, 16), :]
                first = jnp.where(low, even, pltpu.roll(odd, 64, 1))
                second = jnp.where(low, pltpu.roll(even, 64, 1), odd)
                at = slice(j * 128, j * 128 + 128)
                out_ref[to + 2 * t, :, at] = first.astype(out_ref.dtype)
                out_ref[to + 2 * t + 1, :, at] = second.astype(out_ref.dtype)
        return carry

    lax.fori_loop(0, 16, emit, 0)

    def emit_partner(v, carry):
        for t in range(4):
            tiles = [
                scratch[t, pl.ds(pl.multiple_of((128 + s * 8 + v) * 16, 16), 16), :]
                for s in range(4)
            ]
            for g in range(4):
                total = jnp.zeros((16, 128), jnp.float32)
                for s in range(4):
                    by = (s - g) * 32 % 128
                    tile = pltpu.roll(tiles[s], by, 1) if by else tiles[s]
                    total = jnp.where(lane // 32 == s, tile, total)
                out_ref[(t * 4 + g) * 8 + v, :, 512:640] = total.astype(out_ref.dtype)
        return carry

    lax.fori_loop(0, 8, emit_partner, 0)


def transformed(pair_order, owner_table, three_index, virt_coeff):
    vmem = pl.BlockSpec(memory_space=pltpu.VMEM)
    return pl.pallas_call(
        half_kernel,
        in_specs=[pl.BlockSpec(memory_space=pltpu.SMEM)] + [vmem] * 3,
        out_specs=vmem,
        out_shape=jax.ShapeDtypeStruct((128, 16, 640), jnp.bfloat16),
        scratch_shapes=[
            pltpu.VMEM((4, 160 * 16, 128), jnp.float32),
            pltpu.VMEM((160, 128), jnp.float32),
        ],
        name="half",
    )(pair_order, owner_table.reshape(1, 128), three_index, virt_coeff)


def fit_kernel(table_ref, rows_ref, *refs, first, width, outs):
    parts, out_refs = refs[:8], refs[8:8 + outs]
    rows, metric, sems, row_sem = refs[8 + outs:]
    take = pltpu.make_async_copy(rows_ref.at[:, pl.ds(first, width)], rows, row_sem)
    take.start()
    for buf in range(8):

        def start(j, carry, buf=buf):
            row = pl.multiple_of(table_ref[buf * 16 + j] * 16, 16)
            pltpu.make_async_copy(
                parts[buf].at[pl.ds(pl.multiple_of(j * 16, 16), 16)],
                metric.at[pl.ds(row, 16)],
                sems.at[buf],
            ).start()
            return carry

        lax.fori_loop(0, 16, start, 0)
    take.wait()
    left = rows[...].T
    for buf in range(8):
        pltpu.make_async_copy(parts[buf], metric.at[pl.ds(0, 256)], sems.at[buf]).wait()
    each = width // outs
    for block in range(4):
        at = slice(block * 512, block * 512 + 512)
        fitted = lax.dot_general(
            left, metric[at, :], (((1,), (1,)), ((), ())), preferred_element_type=jnp.float32
        ).astype(jnp.bfloat16)
        for i in range(outs):
            out_refs[i][:, at] = fitted[i * each:i * each + each]


def fit(table, owned, parts, first, width, outs):
    vmem = pl.BlockSpec(memory_space=pltpu.VMEM)
    shape = jax.ShapeDtypeStruct((width // outs, 2048), jnp.bfloat16)

    def body(*refs):
        fit_kernel(*refs, first=first, width=width, outs=outs)

    return pl.pallas_call(
        body,
        in_specs=[pl.BlockSpec(memory_space=pltpu.SMEM)] + [pl.BlockSpec(memory_space=pl.ANY)] * 9,
        out_specs=[vmem] * outs,
        out_shape=[shape] * outs,
        scratch_shapes=[
            pltpu.VMEM((2048, width), jnp.bfloat16),
            pltpu.VMEM((2048, 2048), jnp.bfloat16),
            pltpu.SemaphoreType.DMA((8,)),
            pltpu.SemaphoreType.DMA,
        ],
        name="fit_own" if outs == 1 else "fit_partner",
    )(table, owned, *parts)


def pair_kernel(own_ref, row_ref, col_ref, *refs, groups, chained):
    count = sum(groups)
    if chained:
        total_ref, refs = refs[0], refs[1:]
    parts, (out_ref, own, buf, sems, more) = refs[:count], refs[count:]
    take = pltpu.make_async_copy(own_ref, own, more.at[0])
    take.start()
    copies, at = [], 0
    for i, part in enumerate(parts):
        rows = part.shape[0]
        copies.append(pltpu.make_async_copy(part, buf.at[pl.ds(at, rows)], sems.at[i]))
        copies[-1].start()
        at += rows
    if chained:
        total = pltpu.make_async_copy(total_ref, out_ref, more.at[1])
        total.start()
    row = row_ref[:, :1]
    take.wait()
    start, piece = 0, 0
    for block, size in enumerate(groups):
        rows = 0
        for _ in range(size):
            copies[piece].wait()
            rows += parts[piece].shape[0]
            piece += 1
        part = buf[start:start + rows, :]
        pair = lax.dot_general(
            own[...], part, (((1,), (1,)), ((), ())), preferred_element_type=jnp.float32
        )
        amp = (pair / (row + col_ref[:, start:start + rows])).astype(jnp.bfloat16)
        if block == 0 and chained:
            total.wait()
        term = jnp.dot(amp, part, preferred_element_type=jnp.float32)
        if block == 0 and not chained:
            out_ref[...] = term
        else:
            out_ref[...] += term
        start += rows


def paired(own, row, col, groups, total=None):
    vmem, hbm = pl.BlockSpec(memory_space=pltpu.VMEM), pl.BlockSpec(memory_space=pl.ANY)
    parts = [part for group in groups for part in group]
    chained = total is not None
    more = [total] if chained else []
    rows = sum(part.shape[0] for part in parts)
    sizes = tuple(len(group) for group in groups)

    def body(*refs):
        pair_kernel(*refs, groups=sizes, chained=chained)

    return pl.pallas_call(
        body,
        in_specs=[hbm, vmem, vmem] + [hbm] * (len(parts) + len(more)),
        out_specs=vmem,
        out_shape=jax.ShapeDtypeStruct((512, 2048), jnp.float32),
        scratch_shapes=[
            pltpu.VMEM((512, 2048), jnp.bfloat16),
            pltpu.VMEM((rows, 2048), jnp.bfloat16),
            pltpu.SemaphoreType.DMA((len(parts),)),
            pltpu.SemaphoreType.DMA((2,)),
        ],
        name="pair_more" if chained else "pair",
    )(own, row, col, *more, *parts)


def energies(me, owner_table, pair_order, occ_energy, vir_energy):
    occ_idx, vir_idx = me // 8, me % 8
    one_hot = (owner_table[:, None] == jnp.arange(128, dtype=jnp.int32)[None, :]).astype(jnp.float32)
    eps = jnp.dot(one_hot, occ_energy, precision=lax.Precision.HIGHEST)
    own_eps = lax.dynamic_slice_in_dim(eps, occ_idx * 8, 8, 0)
    block_eps = lax.dynamic_slice_in_dim(vir_energy, vir_idx * 64, 64, 0)
    row = (own_eps[:, None] - block_eps[None, :]).reshape(512, 1)
    row = jnp.broadcast_to(row, (512, 128))
    chunks, steps = partner_table()
    chunk = lax.dynamic_slice_in_dim(jnp.asarray(chunks), me, 1, 0).reshape(64)
    pick = (chunk[:, None] == jnp.arange(16, dtype=jnp.int32)[None, :]).astype(jnp.float32)
    vir_rows = jnp.dot(pick, vir_energy.reshape(16, 32), precision=lax.Precision.HIGHEST)
    partner_eps = jnp.concatenate(
        [lax.dynamic_slice_in_dim(eps, pair_order[s] * 8 + vir_idx, 1, 0) for s in range(4)]
    )
    which = jnp.asarray((steps[:, None] == np.arange(4)[None, :]).astype(np.float32))
    eps_rows = jnp.dot(which, partner_eps[:, None], precision=lax.Precision.HIGHEST)
    return row, (eps_rows - vir_rows).reshape(1, 2048)


def whole(three_index, virt_coeff, metric_root, owner_table, pair_order, occ_energy, vir_energy):
    me = lax.axis_index("occ") * 8 + lax.axis_index("vir")
    metric_parts = gathered_metric(metric_root)
    sent = transformed(pair_order, owner_table, three_index, virt_coeff)
    owned = lax.all_to_all(sent, AXES, split_axis=0, concat_axis=0, tiled=True)
    owned = owned.reshape(2048, 640)

    row, col = energies(me, owner_table, pair_order, occ_energy, vir_energy)
    table = lax.dynamic_slice_in_dim(jnp.asarray(metric_table()), me, 1, 0).reshape(128)
    owned, row, col, table = lax.optimization_barrier((owned, row, col, table))

    early, late = fit(table, owned, metric_parts, 512, 128, 2)
    (own,) = fit(table, owned, metric_parts, 0, 512, 1)

    ydim, zdim = ("y", "y"), ("z", "z")
    early = jnp.concatenate([early, shifted(early, zdim, 2)], axis=0)
    late = jnp.concatenate([late] + [shifted(late, ydim, by) for by in (1, 2, 3)], axis=0)
    have = {("e", 0): early, ("l", 0): late}
    for by in (2, 1, 3):
        have["e", by] = shifted(early, ydim, by)
    have["l", 1] = shifted(late, zdim, 2)
    pieces = {}
    for (kind, by), part in have.items():
        pieces[kind, by, 0] = part
        pieces[kind, by, 1] = swapped(part)

    first = [[pieces[key] for key in group] for group in FIRST]
    second = [[pieces[key] for key in group] for group in SECOND]
    density = paired(own, row, col[:, :768], first)
    density = paired(own, row, col[:, 768:], second, density)
    return density.reshape(8, 64, 2048)


def solution(mesh):
    placed = (P(AXES, None, None), P(), P(AXES, None), P(), P(), P(), P())
    return jax.shard_map(
        whole, mesh=mesh, in_specs=placed, out_specs=P("occ", "vir", None), check_vma=False
    )
```

```python
import numpy as np
import jax
import jax.numpy as jnp
from jax import lax
from jax.experimental import pallas as pl
from jax.experimental.pallas import tpu as pltpu
from jax.sharding import PartitionSpec as P


AXES = ("occ", "vir")
SIZE = {"x": 4, "y": 4, "z": 4}
ORDER = (("z", "x", "y"), ("y", "z", "x"))


def line(p):
    return ((p["y"] * 2 + p["z"] // 2) * 2 + p["c"]) * 8 + p["x"] * 2 + p["z"] % 2


def places():
    return [
        dict(x=x, y=y, z=z, c=c)
        for x in range(4)
        for y in range(4)
        for z in range(4)
        for c in range(2)
    ]


def moved(p, dim, by):
    q = dict(p)
    q[dim] = (q[dim] + by) % SIZE[dim]
    return q


def shifted(value, dims, by):
    pairs = [(line(p), line(moved(p, dims[p["c"]], by))) for p in places()]
    return lax.ppermute(value, AXES, pairs)


def swapped(value):
    pairs = [(line(p), line(dict(p, c=1 - p["c"]))) for p in places()]
    return lax.ppermute(value, AXES, pairs)


def metric_table():
    table = np.zeros((128, 8, 16), np.int32)
    for p in places():
        for buf in range(8):
            core = p["c"] if buf < 4 else 1 - p["c"]
            first, second, third = ORDER[core]
            for k2 in range(4):
                for k1 in range(4):
                    q = dict(p, c=core)
                    for dim, by in ((third, buf % 4), (second, k2), (first, k1)):
                        q = moved(q, dim, -by)
                    table[line(p), buf, k2 * 4 + k1] = line(q)
    return table


FIRST = ((("l", 0, 0), ("e", 0, 0), ("e", 0, 1)), (("l", 0, 1),))
SECOND = (
    (("e", 1, 0), ("e", 3, 0), ("e", 1, 1), ("e", 3, 1)),
    (("e", 2, 0), ("e", 2, 1), ("l", 1, 0)),
    (("l", 1, 1),),
)


def partner_table():
    chunk = np.zeros((128, 64), np.int32)
    step = np.zeros((64,), np.int32)
    for p in places():
        at = 0
        for kind, by, other in [key for group in FIRST + SECOND for key in group]:
            core = 1 - p["c"] if other else p["c"]
            if kind == "e":
                inner = [(by, kz, s) for kz in range(2) for s in (0, 1)]
            else:
                inner = [(ky, by, s) for ky in range(4) for s in (2, 3)]
            for ky, kz, s in inner:
                q = moved(moved(dict(p, c=core), "y", -ky), "z", 2 * kz)
                chunk[line(p), at] = line(q) // 8
                step[at] = s
                at += 1
    return chunk, step


def gathered_metric(rows):
    for stage in (0, 1):
        dims = (ORDER[0][stage], ORDER[1][stage])
        got = [shifted(rows, dims, by) for by in (1, 2, 3)]
        rows = jnp.concatenate([rows] + got, axis=0)
    dims = (ORDER[0][2], ORDER[1][2])
    mine = [rows] + [shifted(rows, dims, by) for by in (1, 2, 3)]
    return mine + [swapped(part) for part in mine]


def half_kernel(order_ref, owner_ref, ints_ref, coeff_ref, part_ref, own_ref, *scratches):
    ints, scratch, pick_ref, part, own, in_sems, out_sems = scratches
    takes = [
        pltpu.make_async_copy(
            ints_ref.at[pl.ds(c * 4, 4)], ints.at[pl.ds(c * 4, 4)], in_sems.at[c]
        )
        for c in range(4)
    ]
    for take in takes:
        take.start()
    owners = jnp.broadcast_to(owner_ref[...].astype(jnp.float32), (128, 128)).T
    orbital = lax.broadcasted_iota(jnp.int32, (128, 128), 1).astype(jnp.float32)
    pick_ref[0:128, :] = jnp.where(owners == orbital, 1.0, 0.0)
    for s in range(4):
        first = pl.multiple_of(order_ref[s] * 8, 8)
        pick_ref[128 + 8 * s:136 + 8 * s, :] = pick_ref[pl.ds(first, 8), :]
    pick = pick_ref[...].astype(jnp.bfloat16)

    for c in range(4):
        takes[c].wait()
        half = jnp.dot(
            ints[c * 4:c * 4 + 4].reshape(512, 640),
            coeff_ref[...],
            preferred_element_type=jnp.float32,
        ).astype(jnp.bfloat16)
        for i in range(4):
            rows = jnp.dot(
                pick, half[i * 128:i * 128 + 128], preferred_element_type=jnp.float32
            )
            for t in range(4):
                at = pl.ds(c * 4 + i, 160, stride=16)
                scratch.at[t][at, :] = rows[:, t * 128:t * 128 + 128]

    lane = lax.broadcasted_iota(jnp.int32, (16, 128), 1)
    low = lane < 64

    def emit_partner(v, carry):
        for t in range(4):
            tiles = [
                scratch[t, pl.ds(pl.multiple_of((128 + s * 8 + v) * 16, 16), 16), :]
                for s in range(4)
            ]
            for g in range(4):
                total = jnp.zeros((16, 128), jnp.float32)
                for s in range(4):
                    by = (s - g) * 32 % 128
                    tile = pltpu.roll(tiles[s], by, 1) if by else tiles[s]
                    total = jnp.where(lane // 32 == s, tile, total)
                part[(t * 4 + g) * 8 + v] = total.astype(part.dtype)
        return carry

    lax.fori_loop(0, 8, emit_partner, 0)
    send_part = pltpu.make_async_copy(part, part_ref, out_sems.at[0])
    send_part.start()

    def emit(group, carry):
        first_row = pl.multiple_of(group * 128, 128)
        to = pl.multiple_of(group * 8, 8)
        for t in range(4):
            for j in range(4):
                even = scratch[t, pl.ds(first_row + 32 * j, 16), :]
                odd = scratch[t, pl.ds(first_row + 32 * j + 16, 16), :]
                first = jnp.where(low, even, pltpu.roll(odd, 64, 1))
                second = jnp.where(low, pltpu.roll(even, 64, 1), odd)
                at = slice(j * 128, j * 128 + 128)
                own[to + 2 * t, :, at] = first.astype(own.dtype)
                own[to + 2 * t + 1, :, at] = second.astype(own.dtype)
        return carry

    sends = [
        pltpu.make_async_copy(
            own.at[pl.ds(h * 64, 64)], own_ref.at[pl.ds(h * 64, 64)], out_sems.at[1 + h]
        )
        for h in range(2)
    ]
    for h in range(2):
        lax.fori_loop(8 * h, 8 * h + 8, emit, 0)
        sends[h].start()
    send_part.wait()
    for send in sends:
        send.wait()


def transformed(pair_order, owner_table, three_index, virt_coeff):
    vmem, hbm = pl.BlockSpec(memory_space=pltpu.VMEM), pl.BlockSpec(memory_space=pl.ANY)
    part = jax.ShapeDtypeStruct((128, 16, 128), jnp.bfloat16)
    own = jax.ShapeDtypeStruct((128, 16, 512), jnp.bfloat16)
    return pl.pallas_call(
        half_kernel,
        in_specs=[pl.BlockSpec(memory_space=pltpu.SMEM), vmem, hbm, vmem],
        out_specs=[hbm, hbm],
        out_shape=[part, own],
        scratch_shapes=[
            pltpu.VMEM((16, 128, 640), jnp.bfloat16),
            pltpu.VMEM((4, 160 * 16, 128), jnp.float32),
            pltpu.VMEM((160, 128), jnp.float32),
            pltpu.VMEM(part.shape, part.dtype),
            pltpu.VMEM(own.shape, own.dtype),
            pltpu.SemaphoreType.DMA((4,)),
            pltpu.SemaphoreType.DMA((3,)),
        ],
        name="half",
    )(pair_order, owner_table.reshape(1, 128), three_index, virt_coeff)


def fit_kernel(table_ref, rows_ref, *refs, width, outs):
    parts, out_refs = refs[:8], refs[8:8 + outs]
    rows, metric, sems, row_sem = refs[8 + outs:]
    take = pltpu.make_async_copy(rows_ref, rows, row_sem)
    take.start()
    for buf in range(8):

        def start(j, carry, buf=buf):
            row = pl.multiple_of(table_ref[buf * 16 + j] * 16, 16)
            pltpu.make_async_copy(
                parts[buf].at[pl.ds(pl.multiple_of(j * 16, 16), 16)],
                metric.at[pl.ds(row, 16)],
                sems.at[buf],
            ).start()
            return carry

        lax.fori_loop(0, 16, start, 0)
    take.wait()
    left = rows[...].T
    for buf in range(8):
        pltpu.make_async_copy(parts[buf], metric.at[pl.ds(0, 256)], sems.at[buf]).wait()
    each = width // outs
    for block in range(4):
        at = slice(block * 512, block * 512 + 512)
        fitted = lax.dot_general(
            left, metric[at, :], (((1,), (1,)), ((), ())), preferred_element_type=jnp.float32
        ).astype(jnp.bfloat16)
        for i in range(outs):
            out_refs[i][:, at] = fitted[i * each:i * each + each]


def fit(table, owned, parts, outs):
    width = owned.shape[1]
    vmem = pl.BlockSpec(memory_space=pltpu.VMEM)
    shape = jax.ShapeDtypeStruct((width // outs, 2048), jnp.bfloat16)

    def body(*refs):
        fit_kernel(*refs, width=width, outs=outs)

    return pl.pallas_call(
        body,
        in_specs=[pl.BlockSpec(memory_space=pltpu.SMEM)] + [pl.BlockSpec(memory_space=pl.ANY)] * 9,
        out_specs=[vmem] * outs,
        out_shape=[shape] * outs,
        scratch_shapes=[
            pltpu.VMEM((2048, width), jnp.bfloat16),
            pltpu.VMEM((2048, 2048), jnp.bfloat16),
            pltpu.SemaphoreType.DMA((8,)),
            pltpu.SemaphoreType.DMA,
        ],
        name="fit_own" if outs == 1 else "fit_partner",
    )(table, owned, *parts)


def pair_kernel(own_ref, row_ref, col_ref, *refs, groups, chained):
    count = sum(groups)
    if chained:
        total_ref, refs = refs[0], refs[1:]
    parts, (out_ref, own, buf, sems, more) = refs[:count], refs[count:]
    take = pltpu.make_async_copy(own_ref, own, more.at[0])
    take.start()
    copies, at = [], 0
    for i, part in enumerate(parts):
        rows = part.shape[0]
        copies.append(pltpu.make_async_copy(part, buf.at[pl.ds(at, rows)], sems.at[i]))
        copies[-1].start()
        at += rows
    if chained:
        total = pltpu.make_async_copy(total_ref, out_ref, more.at[1])
        total.start()
    row = row_ref[:, :1]
    take.wait()
    start, piece = 0, 0
    for block, size in enumerate(groups):
        rows = 0
        for _ in range(size):
            copies[piece].wait()
            rows += parts[piece].shape[0]
            piece += 1
        part = buf[start:start + rows, :]
        pair = lax.dot_general(
            own[...], part, (((1,), (1,)), ((), ())), preferred_element_type=jnp.float32
        )
        amp = (pair / (row + col_ref[:, start:start + rows])).astype(jnp.bfloat16)
        if block == 0 and chained:
            total.wait()
        term = jnp.dot(amp, part, preferred_element_type=jnp.float32)
        if block == 0 and not chained:
            out_ref[...] = term
        else:
            out_ref[...] += term
        start += rows


def paired(own, row, col, groups, total=None):
    vmem, hbm = pl.BlockSpec(memory_space=pltpu.VMEM), pl.BlockSpec(memory_space=pl.ANY)
    parts = [part for group in groups for part in group]
    chained = total is not None
    more = [total] if chained else []
    rows = sum(part.shape[0] for part in parts)
    sizes = tuple(len(group) for group in groups)

    def body(*refs):
        pair_kernel(*refs, groups=sizes, chained=chained)

    return pl.pallas_call(
        body,
        in_specs=[hbm, vmem, vmem] + [hbm] * (len(parts) + len(more)),
        out_specs=vmem,
        out_shape=jax.ShapeDtypeStruct((512, 2048), jnp.float32),
        scratch_shapes=[
            pltpu.VMEM((512, 2048), jnp.bfloat16),
            pltpu.VMEM((rows, 2048), jnp.bfloat16),
            pltpu.SemaphoreType.DMA((len(parts),)),
            pltpu.SemaphoreType.DMA((2,)),
        ],
        name="pair_more" if chained else "pair",
    )(own, row, col, *more, *parts)


def energies(me, owner_table, pair_order, occ_energy, vir_energy):
    occ_idx, vir_idx = me // 8, me % 8
    one_hot = (owner_table[:, None] == jnp.arange(128, dtype=jnp.int32)[None, :]).astype(jnp.float32)
    eps = jnp.dot(one_hot, occ_energy, precision=lax.Precision.HIGHEST)
    own_eps = lax.dynamic_slice_in_dim(eps, occ_idx * 8, 8, 0)
    block_eps = lax.dynamic_slice_in_dim(vir_energy, vir_idx * 64, 64, 0)
    row = (own_eps[:, None] - block_eps[None, :]).reshape(512, 1)
    row = jnp.broadcast_to(row, (512, 128))
    chunks, steps = partner_table()
    chunk = lax.dynamic_slice_in_dim(jnp.asarray(chunks), me, 1, 0).reshape(64)
    pick = (chunk[:, None] == jnp.arange(16, dtype=jnp.int32)[None, :]).astype(jnp.float32)
    vir_rows = jnp.dot(pick, vir_energy.reshape(16, 32), precision=lax.Precision.HIGHEST)
    partner_eps = jnp.concatenate(
        [lax.dynamic_slice_in_dim(eps, pair_order[s] * 8 + vir_idx, 1, 0) for s in range(4)]
    )
    which = jnp.asarray((steps[:, None] == np.arange(4)[None, :]).astype(np.float32))
    eps_rows = jnp.dot(which, partner_eps[:, None], precision=lax.Precision.HIGHEST)
    return row, (eps_rows - vir_rows).reshape(1, 2048)


def whole(three_index, virt_coeff, metric_root, owner_table, pair_order, occ_energy, vir_energy):
    me = lax.axis_index("occ") * 8 + lax.axis_index("vir")
    metric_parts = gathered_metric(metric_root)
    part, own = transformed(pair_order, owner_table, three_index, virt_coeff)
    part = lax.all_to_all(part, AXES, split_axis=0, concat_axis=0, tiled=True)
    own = lax.all_to_all(own, AXES, split_axis=0, concat_axis=0, tiled=True)
    part, own = part.reshape(2048, 128), own.reshape(2048, 512)

    row, col = energies(me, owner_table, pair_order, occ_energy, vir_energy)
    table = lax.dynamic_slice_in_dim(jnp.asarray(metric_table()), me, 1, 0).reshape(128)
    part, row, col, table = lax.optimization_barrier((part, row, col, table))

    early, late = fit(table, part, metric_parts, 2)
    (own,) = fit(table, own, metric_parts, 1)

    ydim, zdim = ("y", "y"), ("z", "z")
    early = jnp.concatenate([early, shifted(early, zdim, 2)], axis=0)
    late = jnp.concatenate([late] + [shifted(late, ydim, by) for by in (1, 2, 3)], axis=0)
    have = {("e", 0): early, ("l", 0): late}
    for by in (2, 1, 3):
        have["e", by] = shifted(early, ydim, by)
    have["l", 1] = shifted(late, zdim, 2)
    pieces = {}
    for (kind, by), part in have.items():
        pieces[kind, by, 0] = part
        pieces[kind, by, 1] = swapped(part)

    first = [[pieces[key] for key in group] for group in FIRST]
    second = [[pieces[key] for key in group] for group in SECOND]
    density = paired(own, row, col[:, :768], first)
    density = paired(own, row, col[:, 768:], second, density)
    return density.reshape(8, 64, 2048)


def solution(mesh):
    placed = (P(AXES, None, None), P(), P(AXES, None), P(), P(), P(), P())
    return jax.shard_map(
        whole, mesh=mesh, in_specs=placed, out_specs=P("occ", "vir", None), check_vma=False
    )
```

```python
import numpy as np
import jax
import jax.numpy as jnp
from jax import lax
from jax.experimental import pallas as pl
from jax.experimental.pallas import tpu as pltpu
from jax.sharding import PartitionSpec as P


AXES = ("occ", "vir")
SIZE = {"x": 4, "y": 4, "z": 4}
ORDER = (("z", "x", "y"), ("y", "z", "x"))


def line(p):
    return ((p["y"] * 2 + p["z"] // 2) * 2 + p["c"]) * 8 + p["x"] * 2 + p["z"] % 2


def places():
    return [
        dict(x=x, y=y, z=z, c=c)
        for x in range(4)
        for y in range(4)
        for z in range(4)
        for c in range(2)
    ]


def moved(p, dim, by):
    q = dict(p)
    q[dim] = (q[dim] + by) % SIZE[dim]
    return q


def shifted(value, dims, by):
    pairs = [(line(p), line(moved(p, dims[p["c"]], by))) for p in places()]
    return lax.ppermute(value, AXES, pairs)


def swapped(value):
    pairs = [(line(p), line(dict(p, c=1 - p["c"]))) for p in places()]
    return lax.ppermute(value, AXES, pairs)


def metric_table():
    table = np.zeros((128, 129), np.int32)
    for p in places():
        for buf in range(8):
            core = p["c"] if buf < 4 else 1 - p["c"]
            first, second, third = ORDER[core]
            for k2 in range(4):
                for k1 in range(4):
                    q = dict(p, c=core)
                    for dim, by in ((third, buf % 4), (second, k2), (first, k1)):
                        q = moved(q, dim, -by)
                    block = line(q) // 16 * 8 + line(q) % 8 + (buf // 4) * 64
                    table[line(p), buf * 16 + k2 * 4 + k1] = block
        table[line(p), 128] = p["c"]
    return table


def gathered_metric(rows):
    for stage in (0, 1):
        dims = (ORDER[0][stage], ORDER[1][stage])
        got = [shifted(rows, dims, by) for by in (1, 2, 3)]
        rows = jnp.concatenate([rows] + got, axis=0)
    dims = (ORDER[0][2], ORDER[1][2])
    mine = [rows] + [shifted(rows, dims, by) for by in (1, 2, 3)]
    return mine, [swapped(part) for part in mine]


PITCH = 168


def half_kernel(order_ref, owner_ref, ints_ref, coeff_ref, part_ref, own_ref, *scratches):
    ints, scratch, pick_ref, part, own, in_sems, out_sems = scratches
    takes = [
        pltpu.make_async_copy(
            ints_ref.at[pl.ds(c * 4, 4)], ints.at[pl.ds(c * 4, 4)], in_sems.at[c]
        )
        for c in range(4)
    ]
    for take in takes:
        take.start()
    owners = jnp.broadcast_to(owner_ref[...].astype(jnp.float32), (128, 128)).T
    orbital = lax.broadcasted_iota(jnp.int32, (128, 128), 1).astype(jnp.float32)
    pick_ref[0:128, :] = jnp.where(owners == orbital, 1.0, 0.0)
    for s in range(4):
        first = pl.multiple_of(order_ref[s] * 8, 8)
        pick_ref[128 + 8 * s:136 + 8 * s, :] = pick_ref[pl.ds(first, 8), :]
    pick = pick_ref[...].astype(jnp.bfloat16)

    for c in range(4):
        takes[c].wait()
        half = jnp.dot(
            ints[c * 4:c * 4 + 4].reshape(512, 640),
            coeff_ref[...],
            preferred_element_type=jnp.float32,
        ).astype(jnp.bfloat16)
        for i in range(4):
            rows = jnp.dot(
                pick, half[i * 128:i * 128 + 128], preferred_element_type=jnp.float32
            )
            at = (c * 4 + i) * PITCH
            for t in range(4):
                scratch[t, at:at + 160, :] = rows[:, t * 128:t * 128 + 128]

    lane = lax.broadcasted_iota(jnp.int32, (16, 128), 1)
    low = lane < 64

    def rows_of(t, position):
        return scratch.at[t][pl.ds(position, 16, stride=PITCH), :]

    def emit_partner(v, carry):
        for t in range(4):
            for s in range(4):
                tile = rows_of(t, 128 + s * 8 + v).astype(part.dtype)
                for far in range(2):
                    for z in range(2):
                        owner = ((t // 2 + 2 * far) * 2 + z) * 2 + t % 2
                        part[owner * 8 + v, :, s * 128:s * 128 + 128] = tile
        return carry

    lax.fori_loop(0, 8, emit_partner, 0)
    send_part = pltpu.make_async_copy(part, part_ref, out_sems.at[0])
    send_part.start()

    def emit(group, carry):
        to = pl.multiple_of(group * 8, 8)
        for t in range(4):
            for j in range(4):
                even = rows_of(t, group * 8 + 2 * j)
                odd = rows_of(t, group * 8 + 2 * j + 1)
                first = jnp.where(low, even, pltpu.roll(odd, 64, 1))
                second = jnp.where(low, pltpu.roll(even, 64, 1), odd)
                at = slice(j * 128, j * 128 + 128)
                own[to + 2 * t, :, at] = first.astype(own.dtype)
                own[to + 2 * t + 1, :, at] = second.astype(own.dtype)
        return carry

    sends = [
        pltpu.make_async_copy(
            own.at[pl.ds(h * 64, 64)], own_ref.at[pl.ds(h * 64, 64)], out_sems.at[1 + h]
        )
        for h in range(2)
    ]
    for h in range(2):
        lax.fori_loop(8 * h, 8 * h + 8, emit, 0)
        sends[h].start()
    send_part.wait()
    for send in sends:
        send.wait()


def transformed(pair_order, owner_table, three_index, virt_coeff):
    vmem, hbm = pl.BlockSpec(memory_space=pltpu.VMEM), pl.BlockSpec(memory_space=pl.ANY)
    part = jax.ShapeDtypeStruct((128, 16, 512), jnp.bfloat16)
    own = jax.ShapeDtypeStruct((128, 16, 512), jnp.bfloat16)
    return pl.pallas_call(
        half_kernel,
        in_specs=[pl.BlockSpec(memory_space=pltpu.SMEM), vmem, hbm, vmem],
        out_specs=[hbm, hbm],
        out_shape=[part, own],
        scratch_shapes=[
            pltpu.VMEM((16, 128, 640), jnp.bfloat16),
            pltpu.VMEM((4, 16 * PITCH, 128), jnp.float32),
            pltpu.VMEM((160, 128), jnp.float32),
            pltpu.VMEM(part.shape, part.dtype),
            pltpu.VMEM(own.shape, own.dtype),
            pltpu.SemaphoreType.DMA((4,)),
            pltpu.SemaphoreType.DMA((3,)),
        ],
        name="half",
    )(pair_order, owner_table.reshape(1, 128), three_index, virt_coeff)


def place(table_ref, parts, first, metric, sems):
    for i, part in enumerate(parts):

        def start(j, carry, i=i, part=part):
            row = pl.multiple_of(table_ref[(first + i) * 16 + j] * 16, 16)
            pltpu.make_async_copy(
                part.at[pl.ds(pl.multiple_of(j * 16, 16), 16)],
                metric.at[pl.ds(row, 16)],
                sems.at[first + i],
            ).start()
            return carry

        lax.fori_loop(0, 16, start, 0)


def placed(parts, first, metric, sems):
    for i, part in enumerate(parts):
        pltpu.make_async_copy(part, metric.at[pl.ds(0, 256)], sems.at[first + i]).wait()


def fitted(left, metric):
    return lax.dot_general(
        left, metric, (((1,), (1,)), ((), ())), preferred_element_type=jnp.float32
    ).astype(jnp.bfloat16)


def partner_kernel(table_ref, mine_ref, other_ref, *refs):
    parts, outs, (rows, metric, sems, row_sems) = refs[:4], refs[4:8], refs[8:]
    core = table_ref[128]
    takes = [
        pltpu.make_async_copy(mine_ref, rows.at[core], row_sems.at[0]),
        pltpu.make_async_copy(other_ref, rows.at[1 - core], row_sems.at[1]),
    ]
    for take in takes:
        take.start()
    place(table_ref, parts, 0, metric, sems)
    for take in takes:
        take.wait()
    left = [rows[c].T for c in range(2)]
    placed(parts, 0, metric, sems)
    for c in range(2):
        for block in range(2):
            at = slice(block * 512, block * 512 + 512)
            got = fitted(left[c], metric[at, :])
            outs[2 * c][:, at] = got[:256]
            outs[2 * c + 1][:, at] = got[256:]


def partner_fit(table, mine, other, parts):
    smem, vmem = pl.BlockSpec(memory_space=pltpu.SMEM), pl.BlockSpec(memory_space=pltpu.VMEM)
    shape = jax.ShapeDtypeStruct((256, 1024), jnp.bfloat16)
    return pl.pallas_call(
        partner_kernel,
        in_specs=[smem] + [pl.BlockSpec(memory_space=pl.ANY)] * 6,
        out_specs=[vmem] * 4,
        out_shape=[shape] * 4,
        scratch_shapes=[
            pltpu.VMEM((2, 2048, 512), jnp.bfloat16),
            pltpu.VMEM((1024, 2048), jnp.bfloat16),
            pltpu.SemaphoreType.DMA((4,)),
            pltpu.SemaphoreType.DMA((2,)),
        ],
        name="fit_partner",
    )(table, mine, other, *parts)


def fetch(groups, buf, sems):
    found, at, used = [], 0, 0
    for group in groups:
        start, copies = at, []
        for piece in group:
            rows = piece[0].shape[0]
            for half in range(2):
                to = buf.at[pl.ds(at, rows), pl.ds(half * 1024, 1024)]
                copies.append(pltpu.make_async_copy(piece[half], to, sems.at[used]))
                used += 1
            at += rows
        for copy in copies:
            copy.start()
        found.append((start, at, copies))
    return found


def contribute(own, part, row, col, total, fresh, carried, finished):
    pair = lax.dot_general(
        own[...], part, (((1,), (1,)), ((), ())), preferred_element_type=jnp.float32
    )
    amp = (pair / (row + col)).astype(jnp.bfloat16)
    if carried is not None:
        carried[1].wait()
    for chunk in range(4):
        at = slice(chunk * 512, chunk * 512 + 512)
        term = jnp.dot(amp, part[:, at], preferred_element_type=jnp.float32)
        if not fresh:
            term = total[:, at] + term
        if carried is not None:
            term = carried[0][:, at] + term
        total[:, at] = term
        finished(chunk)


def grouped(refs, sizes):
    groups, at = [], 0
    for size in sizes:
        groups.append([refs[at + 2 * i:at + 2 * i + 2] for i in range(size)])
        at += 2 * size
    return groups


def own_kernel(table_ref, rows_ref, row_ref, col_ref, *refs, sizes):
    count = 2 * sum(sizes)
    parts, pieces, refs = refs[:8], refs[8:8 + count], refs[8 + count:]
    own_ref, total_ref, rows, metric, own, buf, total, sems, piece_sems, more = refs
    take = pltpu.make_async_copy(rows_ref, rows, more.at[0])
    take.start()
    place(table_ref, parts, 0, metric, sems)
    groups = fetch(grouped(pieces, sizes), buf, piece_sems)
    take.wait()
    left = rows[...].T
    for half in range(2):
        placed(parts[half * 4:half * 4 + 4], half * 4, metric, sems)
        for block in range(2):
            first = half * 1024 + block * 512
            at = slice(first, first + 512)
            own[:, at] = fitted(left, metric[at, :])
    sends = [pltpu.make_async_copy(own, own_ref, more.at[1])]
    sends[0].start()
    row = row_ref[:, :1]
    for index, (start, stop, copies) in enumerate(groups):
        for copy in copies:
            copy.wait()

        def finished(chunk, last=index == len(groups) - 1):
            if last:
                at = pl.ds(chunk * 512, 512)
                sends.append(
                    pltpu.make_async_copy(total.at[:, at], total_ref.at[:, at], more.at[2 + chunk])
                )
                sends[-1].start()

        contribute(
            own, buf[start:stop, :], row, col_ref[:, start:stop], total,
            index == 0, None, finished,
        )
    for send in sends:
        send.wait()


def own_and_pair(table, own, row, col, parts, groups):
    smem, vmem = pl.BlockSpec(memory_space=pltpu.SMEM), pl.BlockSpec(memory_space=pltpu.VMEM)
    hbm = pl.BlockSpec(memory_space=pl.ANY)
    sizes = tuple(len(group) for group in groups)
    pieces = [half for group in groups for piece in group for half in piece]
    count = sum(piece.shape[0] for piece in pieces) // 2

    def body(*refs):
        own_kernel(*refs, sizes=sizes)

    return pl.pallas_call(
        body,
        in_specs=[smem, hbm, vmem, vmem] + [hbm] * (8 + len(pieces)),
        out_specs=[hbm] * 2,
        out_shape=[
            jax.ShapeDtypeStruct((512, 2048), jnp.bfloat16),
            jax.ShapeDtypeStruct((512, 2048), jnp.float32),
        ],
        scratch_shapes=[
            pltpu.VMEM((2048, 512), jnp.bfloat16),
            pltpu.VMEM((2048, 2048), jnp.bfloat16),
            pltpu.VMEM((512, 2048), jnp.bfloat16),
            pltpu.VMEM((count, 2048), jnp.bfloat16),
            pltpu.VMEM((512, 2048), jnp.float32),
            pltpu.SemaphoreType.DMA((8,)),
            pltpu.SemaphoreType.DMA((len(pieces),)),
            pltpu.SemaphoreType.DMA((6,)),
        ],
        name="own_and_pair",
    )(table, own, row, col, *parts, *pieces)


def pair_kernel(table_ref, own_ref, total_ref, row_ref, col_ref, *refs, sizes):
    count = 2 * sum(sizes)
    pieces, (out_ref, own, buf, before, total, piece_sems, more) = refs[:count], refs[count:]
    core = table_ref[128]
    take = pltpu.make_async_copy(own_ref, own, more.at[0])
    take.start()
    groups = fetch(grouped(pieces, sizes), buf, piece_sems)
    carried = pltpu.make_async_copy(total_ref, before, more.at[1])
    carried.start()
    row = row_ref[:, :1]
    take.wait()
    sends = []

    for index, (start, stop, copies) in enumerate(groups):
        for copy in copies:
            copy.wait()

        def finished(chunk, last=index == len(groups) - 1):
            if last:
                for tile in range(chunk * 4, chunk * 4 + 4):
                    half = core if tile < 8 else 1 - core
                    to = pl.multiple_of(((tile % 8) * 2 + half) * 128, 128)
                    sends.append(
                        pltpu.make_async_copy(
                            total.at[:, pl.ds(tile * 128, 128)],
                            out_ref.at[:, pl.ds(to, 128)],
                            more.at[2 + tile],
                        )
                    )
                    sends[-1].start()

        contribute(
            own, buf[start:stop, :], row, col_ref[:, start:stop], total,
            index == 0, (before, carried) if index == len(groups) - 1 else None, finished,
        )
    for send in sends:
        send.wait()


def paired(table, own, total, row, col, groups):
    smem, vmem = pl.BlockSpec(memory_space=pltpu.SMEM), pl.BlockSpec(memory_space=pltpu.VMEM)
    hbm = pl.BlockSpec(memory_space=pl.ANY)
    sizes = tuple(len(group) for group in groups)
    pieces = [half for group in groups for piece in group for half in piece]
    count = sum(piece.shape[0] for piece in pieces) // 2

    def body(*refs):
        pair_kernel(*refs, sizes=sizes)

    return pl.pallas_call(
        body,
        in_specs=[smem, hbm, hbm, vmem, vmem] + [hbm] * len(pieces),
        out_specs=hbm,
        out_shape=jax.ShapeDtypeStruct((512, 2048), jnp.float32),
        scratch_shapes=[
            pltpu.VMEM((512, 2048), jnp.bfloat16),
            pltpu.VMEM((count, 2048), jnp.bfloat16),
            pltpu.VMEM((512, 2048), jnp.float32),
            pltpu.VMEM((512, 2048), jnp.float32),
            pltpu.SemaphoreType.DMA((len(pieces),)),
            pltpu.SemaphoreType.DMA((18,)),
        ],
        name="pair",
    )(table, own, total, row, col, *pieces)


def energies(me, owner_table, pair_order, occ_energy, vir_energy):
    occ_idx, vir_idx = me // 8, me % 8
    one_hot = (owner_table[:, None] == jnp.arange(128, dtype=jnp.int32)[None, :]).astype(jnp.float32)
    eps = jnp.dot(one_hot, occ_energy, precision=lax.Precision.HIGHEST)
    own_eps = lax.dynamic_slice_in_dim(eps, occ_idx * 8, 8, 0)
    block_eps = lax.dynamic_slice_in_dim(vir_energy, vir_idx * 64, 64, 0)
    row = (own_eps[:, None] - block_eps[None, :]).reshape(512, 1)
    row = jnp.broadcast_to(row, (512, 128))
    partner_eps = jnp.concatenate(
        [lax.dynamic_slice_in_dim(eps, pair_order[s] * 8 + vir_idx, 1, 0) for s in range(4)]
    )
    blocks = partner_eps[None, None, :, None] - vir_energy.reshape(2, 2, 1, 128)
    odd = occ_idx // 4 % 2 == 1
    near = jnp.where(odd, blocks[1], blocks[0])
    far = jnp.where(odd, blocks[0], blocks[1])
    far = far.reshape(2, 2, 2, 128).transpose(1, 0, 2, 3)
    return row, near.reshape(1, 1024), far.reshape(1, 1024)


def whole(three_index, virt_coeff, metric_root, owner_table, pair_order, occ_energy, vir_energy):
    me = lax.axis_index("occ") * 8 + lax.axis_index("vir")
    mine_parts, other_parts = gathered_metric(metric_root)
    part, own = transformed(pair_order, owner_table, three_index, virt_coeff)
    part = lax.all_to_all(part, AXES, split_axis=0, concat_axis=0, tiled=True)
    own = lax.all_to_all(own, AXES, split_axis=0, concat_axis=0, tiled=True)
    part, own = part.reshape(2048, 512), own.reshape(2048, 512)

    row, near, far = energies(me, owner_table, pair_order, occ_energy, vir_energy)
    table = lax.dynamic_slice_in_dim(jnp.asarray(metric_table()), me, 1, 0).reshape(129)
    part, row, near, far, table = lax.optimization_barrier((part, row, near, far, table))
    other = swapped(part)
    here = partner_fit(table, part, other, mine_parts)

    there = []
    for i, by in ((0, 1), (2, 3), (1, 1), (3, 3)):
        there.append(shifted(here[i], ("y", "y"), by))

    def whole_rows(part):
        return part, swapped(part)

    here, there = [whole_rows(part) for part in here], [whole_rows(part) for part in there]
    own, density = own_and_pair(
        table, own, row, near, mine_parts + other_parts, [here[:2], here[2:]]
    )
    density = paired(table, own, density, row, far, [there[:2], there[2:]])
    return density.reshape(8, 64, 2048)


def solution(mesh):
    placed = (P(AXES, None, None), P(), P(AXES, None), P(), P(), P(), P())
    return jax.shard_map(
        whole, mesh=mesh, in_specs=placed, out_specs=P("occ", "vir", None), check_vma=False
    )
```

```python
import numpy as np
import jax
import jax.numpy as jnp
from jax import lax
from jax.experimental import pallas as pl
from jax.experimental.pallas import tpu as pltpu
from jax.sharding import PartitionSpec as P


AXES = ("occ", "vir")
SIZE = {"x": 4, "y": 4, "z": 4}
ORDER = (("z", "x", "y"), ("y", "z", "x"))


def line(p):
    return ((p["y"] * 2 + p["z"] // 2) * 2 + p["c"]) * 8 + p["x"] * 2 + p["z"] % 2


def places():
    return [
        dict(x=x, y=y, z=z, c=c)
        for x in range(4)
        for y in range(4)
        for z in range(4)
        for c in range(2)
    ]


def moved(p, dim, by):
    q = dict(p)
    q[dim] = (q[dim] + by) % SIZE[dim]
    return q


def shifted(value, dims, by):
    pairs = [(line(p), line(moved(p, dims[p["c"]], by))) for p in places()]
    return lax.ppermute(value, AXES, pairs)


def swapped(value):
    pairs = [(line(p), line(dict(p, c=1 - p["c"]))) for p in places()]
    return lax.ppermute(value, AXES, pairs)


def metric_table():
    table = np.zeros((128, 129), np.int32)
    for p in places():
        for buf in range(8):
            core = p["c"] if buf < 4 else 1 - p["c"]
            first, second, third = ORDER[core]
            for k2 in range(4):
                for k1 in range(4):
                    q = dict(p, c=core)
                    for dim, by in ((third, buf % 4), (second, k2), (first, k1)):
                        q = moved(q, dim, -by)
                    block = line(q) // 16 * 8 + line(q) % 8 + (buf // 4) * 64
                    table[line(p), buf * 16 + k2 * 4 + k1] = block
        table[line(p), 128] = p["c"]
    return table


def gathered_metric(rows):
    for stage in (0, 1):
        dims = (ORDER[0][stage], ORDER[1][stage])
        got = [shifted(rows, dims, by) for by in (1, 2, 3)]
        rows = jnp.concatenate([rows] + got, axis=0)
    dims = (ORDER[0][2], ORDER[1][2])
    mine = [rows] + [shifted(rows, dims, by) for by in (1, 2, 3)]
    return mine, [swapped(part) for part in mine]


PITCH = 168


def half_kernel(order_ref, owner_ref, ints_ref, coeff_ref, part_ref, own_ref, *scratches):
    ints, scratch, pick_ref, part, own, in_sems, out_sems = scratches
    takes = [
        pltpu.make_async_copy(
            ints_ref.at[pl.ds(c * 4, 4)], ints.at[pl.ds(c * 4, 4)], in_sems.at[c]
        )
        for c in range(4)
    ]
    for take in takes:
        take.start()
    owners = jnp.broadcast_to(owner_ref[...].astype(jnp.float32), (128, 128)).T
    orbital = lax.broadcasted_iota(jnp.int32, (128, 128), 1).astype(jnp.float32)
    pick_ref[0:128, :] = jnp.where(owners == orbital, 1.0, 0.0)
    for s in range(4):
        first = pl.multiple_of(order_ref[s] * 8, 8)
        pick_ref[128 + 8 * s:136 + 8 * s, :] = pick_ref[pl.ds(first, 8), :]
    pick = pick_ref[...].astype(jnp.bfloat16)

    for c in range(4):
        takes[c].wait()
        half = jnp.dot(
            ints[c * 4:c * 4 + 4].reshape(512, 640),
            coeff_ref[...],
            preferred_element_type=jnp.float32,
        ).astype(jnp.bfloat16)
        for i in range(4):
            rows = jnp.dot(
                pick, half[i * 128:i * 128 + 128], preferred_element_type=jnp.float32
            )
            at = (c * 4 + i) * PITCH
            for t in range(4):
                scratch[t, at:at + 160, :] = rows[:, t * 128:t * 128 + 128]

    lane = lax.broadcasted_iota(jnp.int32, (16, 128), 1)
    low = lane < 64

    def rows_of(t, position):
        return scratch.at[t][pl.ds(position, 16, stride=PITCH), :]

    def emit_partner(v, carry):
        for t in range(4):
            for s in range(4):
                tile = rows_of(t, 128 + s * 8 + v).astype(part.dtype)
                at = slice(s % 2 * 128, s % 2 * 128 + 128)
                for z in range(2):
                    owner = ((t + 2 * z) % 4 * 2 + z) * 2 + s // 2
                    part[owner * 8 + v, :, at] = tile
        return carry

    lax.fori_loop(0, 8, emit_partner, 0)
    send_part = pltpu.make_async_copy(part, part_ref, out_sems.at[0])
    send_part.start()

    def emit(group, carry):
        to = pl.multiple_of(group * 8, 8)
        for t in range(4):
            for j in range(4):
                even = rows_of(t, group * 8 + 2 * j)
                odd = rows_of(t, group * 8 + 2 * j + 1)
                first = jnp.where(low, even, pltpu.roll(odd, 64, 1))
                second = jnp.where(low, pltpu.roll(even, 64, 1), odd)
                at = slice(j * 128, j * 128 + 128)
                own[to + 2 * t, :, at] = first.astype(own.dtype)
                own[to + 2 * t + 1, :, at] = second.astype(own.dtype)
        return carry

    sends = [
        pltpu.make_async_copy(
            own.at[pl.ds(h * 64, 64)], own_ref.at[pl.ds(h * 64, 64)], out_sems.at[1 + h]
        )
        for h in range(2)
    ]
    for h in range(2):
        lax.fori_loop(8 * h, 8 * h + 8, emit, 0)
        sends[h].start()
    send_part.wait()
    for send in sends:
        send.wait()


def transformed(pair_order, owner_table, three_index, virt_coeff):
    vmem, hbm = pl.BlockSpec(memory_space=pltpu.VMEM), pl.BlockSpec(memory_space=pl.ANY)
    part = jax.ShapeDtypeStruct((128, 16, 256), jnp.bfloat16)
    own = jax.ShapeDtypeStruct((128, 16, 512), jnp.bfloat16)
    return pl.pallas_call(
        half_kernel,
        in_specs=[pl.BlockSpec(memory_space=pltpu.SMEM), vmem, hbm, vmem],
        out_specs=[hbm, hbm],
        out_shape=[part, own],
        scratch_shapes=[
            pltpu.VMEM((16, 128, 640), jnp.bfloat16),
            pltpu.VMEM((4, 16 * PITCH, 128), jnp.float32),
            pltpu.VMEM((160, 128), jnp.float32),
            pltpu.VMEM(part.shape, part.dtype),
            pltpu.VMEM(own.shape, own.dtype),
            pltpu.SemaphoreType.DMA((4,)),
            pltpu.SemaphoreType.DMA((3,)),
        ],
        name="half",
    )(pair_order, owner_table.reshape(1, 128), three_index, virt_coeff)


def place(table_ref, parts, first, metric, sems):
    for i, part in enumerate(parts):

        def start(j, carry, i=i, part=part):
            row = pl.multiple_of(table_ref[(first + i) * 16 + j] * 16, 16)
            pltpu.make_async_copy(
                part.at[pl.ds(pl.multiple_of(j * 16, 16), 16)],
                metric.at[pl.ds(row, 16)],
                sems.at[first + i],
            ).start()
            return carry

        lax.fori_loop(0, 16, start, 0)


def placed(parts, first, metric, sems):
    for i, part in enumerate(parts):
        pltpu.make_async_copy(part, metric.at[pl.ds(0, 256)], sems.at[first + i]).wait()


def fitted(left, metric):
    return lax.dot_general(
        left, metric, (((1,), (1,)), ((), ())), preferred_element_type=jnp.float32
    ).astype(jnp.bfloat16)


def partner_kernel(table_ref, mine_ref, other_ref, *refs):
    parts, outs, (rows, metric, sems, row_sems) = refs[:4], refs[4:7], refs[7:]
    core = table_ref[128]
    takes = [
        pltpu.make_async_copy(mine_ref, rows.at[core], row_sems.at[0]),
        pltpu.make_async_copy(other_ref, rows.at[1 - core], row_sems.at[1]),
    ]
    for take in takes:
        take.start()
    place(table_ref, parts, 0, metric, sems)
    for take in takes:
        take.wait()
    left = jnp.concatenate([rows[c].T for c in range(2)], axis=0)
    placed(parts, 0, metric, sems)
    for block in range(2):
        at = slice(block * 512, block * 512 + 512)
        got = fitted(left, metric[at, :])
        outs[0][:, at] = got
        outs[1][:, at] = got[:256]
        outs[2][:, at] = got[256:]


def partner_fit(table, mine, other, parts):
    smem, vmem = pl.BlockSpec(memory_space=pltpu.SMEM), pl.BlockSpec(memory_space=pltpu.VMEM)
    return pl.pallas_call(
        partner_kernel,
        in_specs=[smem] + [pl.BlockSpec(memory_space=pl.ANY)] * 6,
        out_specs=[vmem] * 3,
        out_shape=[jax.ShapeDtypeStruct((rows, 1024), jnp.bfloat16) for rows in (512, 256, 256)],
        scratch_shapes=[
            pltpu.VMEM((2, 2048, 256), jnp.bfloat16),
            pltpu.VMEM((1024, 2048), jnp.bfloat16),
            pltpu.SemaphoreType.DMA((4,)),
            pltpu.SemaphoreType.DMA((2,)),
        ],
        name="fit_partner",
    )(table, mine, other, *parts)


def fetch(groups, buf, sems):
    found, at, used = [], 0, 0
    for group in groups:
        start, copies = at, []
        for piece in group:
            rows = piece[0].shape[0]
            for half in range(2):
                to = buf.at[pl.ds(at, rows), pl.ds(half * 1024, 1024)]
                copies.append(pltpu.make_async_copy(piece[half], to, sems.at[used]))
                used += 1
            at += rows
        for copy in copies:
            copy.start()
        found.append((start, at, copies))
    return found


def contribute(own, part, row, col, total, fresh, carried, finished):
    pair = lax.dot_general(
        own[...], part, (((1,), (1,)), ((), ())), preferred_element_type=jnp.float32
    )
    amp = (pair / (row + col)).astype(jnp.bfloat16)
    if carried is not None:
        carried[1].wait()
    for chunk in range(4):
        at = slice(chunk * 512, chunk * 512 + 512)
        term = jnp.dot(amp, part[:, at], preferred_element_type=jnp.float32)
        if not fresh:
            term = total[:, at] + term
        if carried is not None:
            term = carried[0][:, at] + term
        total[:, at] = term
        finished(chunk)


def grouped(refs, sizes):
    groups, at = [], 0
    for size in sizes:
        groups.append([refs[at + 2 * i:at + 2 * i + 2] for i in range(size)])
        at += 2 * size
    return groups


def own_kernel(table_ref, rows_ref, row_ref, col_ref, *refs, sizes):
    count = 2 * sum(sizes)
    parts, pieces, refs = refs[:8], refs[8:8 + count], refs[8 + count:]
    own_ref, total_ref, metric, own, buf, total, sems, piece_sems, more = refs
    place(table_ref, parts, 0, metric, sems)
    groups = fetch(grouped(pieces, sizes), buf, piece_sems)
    left = rows_ref[...].T
    for half in range(2):
        placed(parts[half * 4:half * 4 + 4], half * 4, metric, sems)
        for block in range(2):
            first = half * 1024 + block * 512
            at = slice(first, first + 512)
            own[:, at] = fitted(left, metric[at, :])
    sends = [pltpu.make_async_copy(own, own_ref, more.at[1])]
    sends[0].start()
    row = row_ref[:, :1]
    for index, (start, stop, copies) in enumerate(groups):
        for copy in copies:
            copy.wait()

        def finished(chunk, last=index == len(groups) - 1):
            if last:
                at = pl.ds(chunk * 512, 512)
                sends.append(
                    pltpu.make_async_copy(total.at[:, at], total_ref.at[:, at], more.at[2 + chunk])
                )
                sends[-1].start()

        contribute(
            own, buf[start:stop, :], row, col_ref[:, start:stop], total,
            index == 0, None, finished,
        )
    for send in sends:
        send.wait()


def own_and_pair(table, own, row, col, parts, groups):
    smem, vmem = pl.BlockSpec(memory_space=pltpu.SMEM), pl.BlockSpec(memory_space=pltpu.VMEM)
    hbm = pl.BlockSpec(memory_space=pl.ANY)
    sizes = tuple(len(group) for group in groups)
    pieces = [half for group in groups for piece in group for half in piece]
    count = sum(piece.shape[0] for piece in pieces) // 2

    def body(*refs):
        own_kernel(*refs, sizes=sizes)

    return pl.pallas_call(
        body,
        in_specs=[smem, vmem, vmem, vmem] + [hbm] * (8 + len(pieces)),
        out_specs=[hbm] * 2,
        out_shape=[
            jax.ShapeDtypeStruct((512, 2048), jnp.bfloat16),
            jax.ShapeDtypeStruct((512, 2048), jnp.float32),
        ],
        scratch_shapes=[
            pltpu.VMEM((2048, 2048), jnp.bfloat16),
            pltpu.VMEM((512, 2048), jnp.bfloat16),
            pltpu.VMEM((count, 2048), jnp.bfloat16),
            pltpu.VMEM((512, 2048), jnp.float32),
            pltpu.SemaphoreType.DMA((8,)),
            pltpu.SemaphoreType.DMA((len(pieces),)),
            pltpu.SemaphoreType.DMA((6,)),
        ],
        name="own_and_pair",
    )(table, own, row, col, *parts, *pieces)


def pair_kernel(table_ref, own_ref, total_ref, row_ref, col_ref, *refs, sizes, final):
    count = 2 * sum(sizes)
    pieces, (out_ref, own, buf, before, total, piece_sems, more) = refs[:count], refs[count:]
    core = table_ref[128]
    take = pltpu.make_async_copy(own_ref, own, more.at[0])
    take.start()
    groups = fetch(grouped(pieces, sizes), buf, piece_sems)
    carried = pltpu.make_async_copy(total_ref, before, more.at[1])
    carried.start()
    row = row_ref[:, :1]
    take.wait()
    sends = []

    for index, (start, stop, copies) in enumerate(groups):
        for copy in copies:
            copy.wait()

        def finished(chunk, last=index == len(groups) - 1):
            if last:
                for tile in range(chunk * 4, chunk * 4 + 4):
                    to = tile * 128
                    if final:
                        half = core if tile < 8 else 1 - core
                        to = pl.multiple_of(((tile % 8) * 2 + half) * 128, 128)
                    sends.append(
                        pltpu.make_async_copy(
                            total.at[:, pl.ds(tile * 128, 128)],
                            out_ref.at[:, pl.ds(to, 128)],
                            more.at[2 + tile],
                        )
                    )
                    sends[-1].start()

        contribute(
            own, buf[start:stop, :], row, col_ref[:, start:stop], total,
            index == 0, (before, carried) if index == len(groups) - 1 else None, finished,
        )
    for send in sends:
        send.wait()


def paired(table, own, total, row, col, groups, final):
    smem, vmem = pl.BlockSpec(memory_space=pltpu.SMEM), pl.BlockSpec(memory_space=pltpu.VMEM)
    hbm = pl.BlockSpec(memory_space=pl.ANY)
    sizes = tuple(len(group) for group in groups)
    pieces = [half for group in groups for piece in group for half in piece]
    count = sum(piece.shape[0] for piece in pieces) // 2

    def body(*refs):
        pair_kernel(*refs, sizes=sizes, final=final)

    return pl.pallas_call(
        body,
        in_specs=[smem, hbm, hbm, vmem, vmem] + [hbm] * len(pieces),
        out_specs=hbm,
        out_shape=jax.ShapeDtypeStruct((512, 2048), jnp.float32),
        scratch_shapes=[
            pltpu.VMEM((512, 2048), jnp.bfloat16),
            pltpu.VMEM((count, 2048), jnp.bfloat16),
            pltpu.VMEM((512, 2048), jnp.float32),
            pltpu.VMEM((512, 2048), jnp.float32),
            pltpu.SemaphoreType.DMA((len(pieces),)),
            pltpu.SemaphoreType.DMA((18,)),
        ],
        name="pair_last" if final else "pair",
    )(table, own, total, row, col, *pieces)


def energies(me, owner_table, pair_order, occ_energy, vir_energy):
    occ_idx, vir_idx = me // 8, me % 8
    one_hot = (owner_table[:, None] == jnp.arange(128, dtype=jnp.int32)[None, :]).astype(jnp.float32)
    eps = jnp.dot(one_hot, occ_energy, precision=lax.Precision.HIGHEST)
    own_eps = lax.dynamic_slice_in_dim(eps, occ_idx * 8, 8, 0)
    block_eps = lax.dynamic_slice_in_dim(vir_energy, vir_idx * 64, 64, 0)
    row = (own_eps[:, None] - block_eps[None, :]).reshape(512, 1)
    row = jnp.broadcast_to(row, (512, 128))
    partner_eps = jnp.concatenate(
        [lax.dynamic_slice_in_dim(eps, pair_order[s] * 8 + vir_idx, 1, 0) for s in range(4)]
    )
    mine = (occ_idx // 4 + occ_idx // 2 % 2 * 2) % 4
    virtuals = jnp.concatenate([vir_energy, vir_energy]).reshape(8, 128)
    virtuals = lax.dynamic_slice_in_dim(virtuals, mine, 4, 0)
    near = partner_eps[:, None] - virtuals[:1]
    beside = partner_eps[None, :, None] - jnp.stack([virtuals[3], virtuals[1]])[:, None, :]
    across = partner_eps[:, None] - virtuals[2:3]
    first = beside[:, :2].reshape(1, 512)
    second = jnp.concatenate([beside[:, 2:].reshape(1, 512), across.reshape(1, 512)], axis=1)
    return row, near.reshape(1, 512), first, second


def whole(three_index, virt_coeff, metric_root, owner_table, pair_order, occ_energy, vir_energy):
    me = lax.axis_index("occ") * 8 + lax.axis_index("vir")
    mine_parts, other_parts = gathered_metric(metric_root)
    part, own = transformed(pair_order, owner_table, three_index, virt_coeff)
    part = lax.all_to_all(part, AXES, split_axis=0, concat_axis=0, tiled=True)
    own = lax.all_to_all(own, AXES, split_axis=0, concat_axis=0, tiled=True)
    part, own = part.reshape(2048, 256), own.reshape(2048, 512)

    energy = energies(me, owner_table, pair_order, occ_energy, vir_energy)
    table = lax.dynamic_slice_in_dim(jnp.asarray(metric_table()), me, 1, 0).reshape(129)
    part, table, *energy = lax.optimization_barrier((part, table, *energy))
    row, near, first, second = energy
    other = swapped(part)
    here, *halves = partner_fit(table, part, other, mine_parts)

    def whole_rows(part):
        return part, swapped(part)

    beside = []
    for half in range(2):
        beside.append([shifted(halves[half], ("y", "y"), by) for by in (1, 3)])
    across = shifted(here, ("z", "z"), 2)
    here = whole_rows(here)
    beside = [[whole_rows(part) for part in beside[i]] for i in range(2)]
    across = whole_rows(across)
    own, density = own_and_pair(table, own, row, near, mine_parts + other_parts, [[here]])
    density = paired(table, own, density, row, first, [beside[0]], False)
    density = paired(table, own, density, row, second, [beside[1], [across]], True)
    return density.reshape(8, 64, 2048)


def solution(mesh):
    placed = (P(AXES, None, None), P(), P(AXES, None), P(), P(), P(), P())
    return jax.shard_map(
        whole, mesh=mesh, in_specs=placed, out_specs=P("occ", "vir", None), check_vma=False
    )
```

```python
import numpy as np
import jax
import jax.numpy as jnp
from jax import lax
from jax.experimental import pallas as pl
from jax.experimental.pallas import tpu as pltpu
from jax.sharding import PartitionSpec as P


AXES = ("occ", "vir")
SIZE = {"x": 4, "y": 4, "z": 4}
ORDER = (("z", "x", "y"), ("y", "z", "x"))


def line(p):
    return ((p["y"] * 2 + p["z"] // 2) * 2 + p["c"]) * 8 + p["x"] * 2 + p["z"] % 2


def places():
    return [
        dict(x=x, y=y, z=z, c=c)
        for x in range(4)
        for y in range(4)
        for z in range(4)
        for c in range(2)
    ]


def moved(p, dim, by):
    q = dict(p)
    q[dim] = (q[dim] + by) % SIZE[dim]
    return q


def shifted(value, dims, by):
    pairs = [(line(p), line(moved(p, dims[p["c"]], by))) for p in places()]
    return lax.ppermute(value, AXES, pairs)


def swapped(value):
    pairs = [(line(p), line(dict(p, c=1 - p["c"]))) for p in places()]
    return lax.ppermute(value, AXES, pairs)


def metric_table():
    table = np.zeros((128, 129), np.int32)
    for p in places():
        for buf in range(8):
            core = p["c"] if buf < 4 else 1 - p["c"]
            first, second, third = ORDER[core]
            for k2 in range(4):
                for k1 in range(4):
                    q = dict(p, c=core)
                    for dim, by in ((third, buf % 4), (second, k2), (first, k1)):
                        q = moved(q, dim, -by)
                    block = line(q) // 16 * 8 + line(q) % 8 + (buf // 4) * 64
                    table[line(p), buf * 16 + k2 * 4 + k1] = block
        table[line(p), 128] = p["c"]
    return table


def gathered_metric(rows):
    for stage in (0, 1):
        dims = (ORDER[0][stage], ORDER[1][stage])
        got = [shifted(rows, dims, by) for by in (1, 2, 3)]
        rows = jnp.concatenate([rows] + got, axis=0)
    dims = (ORDER[0][2], ORDER[1][2])
    mine = [rows] + [shifted(rows, dims, by) for by in (1, 2, 3)]
    return mine, [swapped(part) for part in mine]


PITCH = 168


def half_kernel(order_ref, owner_ref, ints_ref, coeff_ref, part_ref, own_ref, *scratches):
    ints, scratch, pick_ref, part, own, in_sems, out_sems = scratches
    takes = [
        pltpu.make_async_copy(
            ints_ref.at[pl.ds(c * 4, 4)], ints.at[pl.ds(c * 4, 4)], in_sems.at[c]
        )
        for c in range(4)
    ]
    for take in takes:
        take.start()
    owners = jnp.broadcast_to(owner_ref[...].astype(jnp.float32), (128, 128)).T
    orbital = lax.broadcasted_iota(jnp.int32, (128, 128), 1).astype(jnp.float32)
    pick_ref[0:128, :] = jnp.where(owners == orbital, 1.0, 0.0)
    for s in range(4):
        first = pl.multiple_of(order_ref[s] * 8, 8)
        pick_ref[128 + 8 * s:136 + 8 * s, :] = pick_ref[pl.ds(first, 8), :]
    pick = pick_ref[...].astype(jnp.bfloat16)

    for c in range(4):
        takes[c].wait()
        half = jnp.dot(
            ints[c * 4:c * 4 + 4].reshape(512, 640),
            coeff_ref[...],
            preferred_element_type=jnp.float32,
        ).astype(jnp.bfloat16)
        for i in range(4):
            rows = jnp.dot(
                pick, half[i * 128:i * 128 + 128], preferred_element_type=jnp.float32
            )
            at = (c * 4 + i) * PITCH
            for t in range(4):
                scratch[t, at:at + 160, :] = rows[:, t * 128:t * 128 + 128]

    lane = lax.broadcasted_iota(jnp.int32, (16, 128), 1)
    low = lane < 64

    def rows_of(t, position):
        return scratch.at[t][pl.ds(position, 16, stride=PITCH), :]

    def emit_partner(v, carry):
        for t in range(4):
            for s in range(4):
                tile = rows_of(t, 128 + s * 8 + v).astype(part.dtype)
                at = slice(s % 2 * 128, s % 2 * 128 + 128)
                for z in range(2):
                    owner = ((t + 2 * z) % 4 * 2 + z) * 2 + s // 2
                    part[owner * 8 + v, :, at] = tile
        return carry

    lax.fori_loop(0, 8, emit_partner, 0, unroll=2)
    send_part = pltpu.make_async_copy(part, part_ref, out_sems.at[0])
    send_part.start()

    def emit(group, carry):
        to = pl.multiple_of(group * 8, 8)
        for t in range(4):
            for j in range(4):
                even = rows_of(t, group * 8 + 2 * j)
                odd = rows_of(t, group * 8 + 2 * j + 1)
                first = jnp.where(low, even, pltpu.roll(odd, 64, 1))
                second = jnp.where(low, pltpu.roll(even, 64, 1), odd)
                at = slice(j * 128, j * 128 + 128)
                own[to + 2 * t, :, at] = first.astype(own.dtype)
                own[to + 2 * t + 1, :, at] = second.astype(own.dtype)
        return carry

    sends = [
        pltpu.make_async_copy(
            own.at[pl.ds(h * 64, 64)], own_ref.at[pl.ds(h * 64, 64)], out_sems.at[1 + h]
        )
        for h in range(2)
    ]
    for h in range(2):
        lax.fori_loop(8 * h, 8 * h + 8, emit, 0, unroll=2)
        sends[h].start()
    send_part.wait()
    for send in sends:
        send.wait()


def transformed(pair_order, owner_table, three_index, virt_coeff):
    vmem, hbm = pl.BlockSpec(memory_space=pltpu.VMEM), pl.BlockSpec(memory_space=pl.ANY)
    part = jax.ShapeDtypeStruct((128, 16, 256), jnp.bfloat16)
    own = jax.ShapeDtypeStruct((128, 16, 512), jnp.bfloat16)
    return pl.pallas_call(
        half_kernel,
        in_specs=[pl.BlockSpec(memory_space=pltpu.SMEM), vmem, hbm, vmem],
        out_specs=[hbm, hbm],
        out_shape=[part, own],
        scratch_shapes=[
            pltpu.VMEM((16, 128, 640), jnp.bfloat16),
            pltpu.VMEM((4, 16 * PITCH, 128), jnp.float32),
            pltpu.VMEM((160, 128), jnp.float32),
            pltpu.VMEM(part.shape, part.dtype),
            pltpu.VMEM(own.shape, own.dtype),
            pltpu.SemaphoreType.DMA((4,)),
            pltpu.SemaphoreType.DMA((3,)),
        ],
        name="half",
    )(pair_order, owner_table.reshape(1, 128), three_index, virt_coeff)


def place(table_ref, parts, first, metric, sems):
    for i, part in enumerate(parts):

        def start(j, carry, i=i, part=part):
            row = pl.multiple_of(table_ref[(first + i) * 16 + j] * 16, 16)
            pltpu.make_async_copy(
                part.at[pl.ds(pl.multiple_of(j * 16, 16), 16)],
                metric.at[pl.ds(row, 16)],
                sems.at[first + i],
            ).start()
            return carry

        lax.fori_loop(0, 16, start, 0)


def placed(parts, first, metric, sems):
    for i, part in enumerate(parts):
        pltpu.make_async_copy(part, metric.at[pl.ds(0, 256)], sems.at[first + i]).wait()


def fitted(left, metric):
    return lax.dot_general(
        left, metric, (((1,), (1,)), ((), ())), preferred_element_type=jnp.float32
    ).astype(jnp.bfloat16)


def partner_kernel(table_ref, mine_ref, other_ref, *refs):
    parts, outs, (rows, metric, sems, row_sems) = refs[:4], refs[4:7], refs[7:]
    core = table_ref[128]
    takes = [
        pltpu.make_async_copy(mine_ref, rows.at[core], row_sems.at[0]),
        pltpu.make_async_copy(other_ref, rows.at[1 - core], row_sems.at[1]),
    ]
    for take in takes:
        take.start()
    place(table_ref, parts, 0, metric, sems)
    for take in takes:
        take.wait()
    left = jnp.concatenate([rows[c].T for c in range(2)], axis=0)
    placed(parts, 0, metric, sems)
    for block in range(2):
        at = slice(block * 512, block * 512 + 512)
        got = fitted(left, metric[at, :])
        outs[0][:, at] = got
        outs[1][:, at] = got[:256]
        outs[2][:, at] = got[256:]


def partner_fit(table, mine, other, parts):
    smem, vmem = pl.BlockSpec(memory_space=pltpu.SMEM), pl.BlockSpec(memory_space=pltpu.VMEM)
    return pl.pallas_call(
        partner_kernel,
        in_specs=[smem] + [pl.BlockSpec(memory_space=pl.ANY)] * 6,
        out_specs=[vmem] * 3,
        out_shape=[jax.ShapeDtypeStruct((rows, 1024), jnp.bfloat16) for rows in (512, 256, 256)],
        scratch_shapes=[
            pltpu.VMEM((2, 2048, 256), jnp.bfloat16),
            pltpu.VMEM((1024, 2048), jnp.bfloat16),
            pltpu.SemaphoreType.DMA((4,)),
            pltpu.SemaphoreType.DMA((2,)),
        ],
        name="fit_partner",
    )(table, mine, other, *parts)


def fetch(groups, buf, sems):
    found, at, used = [], 0, 0
    for group in groups:
        start, copies = at, []
        for piece in group:
            rows = piece[0].shape[0]
            for half in range(2):
                to = buf.at[pl.ds(at, rows), pl.ds(half * 1024, 1024)]
                copies.append(pltpu.make_async_copy(piece[half], to, sems.at[used]))
                used += 1
            at += rows
        for copy in copies:
            copy.start()
        found.append((start, at, copies))
    return found


def contribute(own, part, row, col, total, fresh, carried, finished):
    pair = lax.dot_general(
        own[...], part, (((1,), (1,)), ((), ())), preferred_element_type=jnp.float32
    )
    amp = (pair / (row + col)).astype(jnp.bfloat16)
    if carried is not None:
        carried[1].wait()
    for chunk in range(4):
        at = slice(chunk * 512, chunk * 512 + 512)
        term = jnp.dot(amp, part[:, at], preferred_element_type=jnp.float32)
        if not fresh:
            term = total[:, at] + term
        if carried is not None:
            term = carried[0][:, at] + term
        total[:, at] = term
        finished(chunk)


def grouped(refs, sizes):
    groups, at = [], 0
    for size in sizes:
        groups.append([refs[at + 2 * i:at + 2 * i + 2] for i in range(size)])
        at += 2 * size
    return groups


def own_kernel(table_ref, rows_ref, row_ref, col_ref, *refs, sizes):
    count = 2 * sum(sizes)
    parts, pieces, refs = refs[:8], refs[8:8 + count], refs[8 + count:]
    own_ref, total_ref, metric, own, buf, total, sems, piece_sems, more = refs
    place(table_ref, parts, 0, metric, sems)
    groups = fetch(grouped(pieces, sizes), buf, piece_sems)
    left = rows_ref[...].T
    for half in range(2):
        placed(parts[half * 4:half * 4 + 4], half * 4, metric, sems)
        for block in range(2):
            first = half * 1024 + block * 512
            at = slice(first, first + 512)
            own[:, at] = fitted(left, metric[at, :])
    sends = [pltpu.make_async_copy(own, own_ref, more.at[1])]
    sends[0].start()
    row = row_ref[:, :1]
    for index, (start, stop, copies) in enumerate(groups):
        for copy in copies:
            copy.wait()

        def finished(chunk, last=index == len(groups) - 1):
            if last:
                at = pl.ds(chunk * 512, 512)
                sends.append(
                    pltpu.make_async_copy(total.at[:, at], total_ref.at[:, at], more.at[2 + chunk])
                )
                sends[-1].start()

        contribute(
            own, buf[start:stop, :], row, col_ref[:, start:stop], total,
            index == 0, None, finished,
        )
    for send in sends:
        send.wait()


def own_and_pair(table, own, row, col, parts, groups):
    smem, vmem = pl.BlockSpec(memory_space=pltpu.SMEM), pl.BlockSpec(memory_space=pltpu.VMEM)
    hbm = pl.BlockSpec(memory_space=pl.ANY)
    sizes = tuple(len(group) for group in groups)
    pieces = [half for group in groups for piece in group for half in piece]
    count = sum(piece.shape[0] for piece in pieces) // 2

    def body(*refs):
        own_kernel(*refs, sizes=sizes)

    return pl.pallas_call(
        body,
        in_specs=[smem, vmem, vmem, vmem] + [hbm] * (8 + len(pieces)),
        out_specs=[hbm] * 2,
        out_shape=[
            jax.ShapeDtypeStruct((512, 2048), jnp.bfloat16),
            jax.ShapeDtypeStruct((512, 2048), jnp.float32),
        ],
        scratch_shapes=[
            pltpu.VMEM((2048, 2048), jnp.bfloat16),
            pltpu.VMEM((512, 2048), jnp.bfloat16),
            pltpu.VMEM((count, 2048), jnp.bfloat16),
            pltpu.VMEM((512, 2048), jnp.float32),
            pltpu.SemaphoreType.DMA((8,)),
            pltpu.SemaphoreType.DMA((len(pieces),)),
            pltpu.SemaphoreType.DMA((6,)),
        ],
        name="own_and_pair",
    )(table, on_chip(own), row, col, *parts, *pieces)


def pair_kernel(table_ref, own_ref, total_ref, row_ref, col_ref, *refs, sizes, final):
    count = 2 * sum(sizes)
    pieces, (out_ref, own, buf, before, total, piece_sems, more) = refs[:count], refs[count:]
    core = table_ref[128]
    take = pltpu.make_async_copy(own_ref, own, more.at[0])
    take.start()
    groups = fetch(grouped(pieces, sizes), buf, piece_sems)
    carried = pltpu.make_async_copy(total_ref, before, more.at[1])
    carried.start()
    row = row_ref[:, :1]
    take.wait()
    sends = []

    for index, (start, stop, copies) in enumerate(groups):
        for copy in copies:
            copy.wait()

        def finished(chunk, last=index == len(groups) - 1):
            if last:
                for tile in range(chunk * 4, chunk * 4 + 4):
                    to = tile * 128
                    if final:
                        half = core if tile < 8 else 1 - core
                        to = pl.multiple_of(((tile % 8) * 2 + half) * 128, 128)
                    sends.append(
                        pltpu.make_async_copy(
                            total.at[:, pl.ds(tile * 128, 128)],
                            out_ref.at[:, pl.ds(to, 128)],
                            more.at[2 + tile],
                        )
                    )
                    sends[-1].start()

        contribute(
            own, buf[start:stop, :], row, col_ref[:, start:stop], total,
            index == 0, (before, carried) if index == len(groups) - 1 else None, finished,
        )
    for send in sends:
        send.wait()


def paired(table, own, total, row, col, groups, final):
    smem, vmem = pl.BlockSpec(memory_space=pltpu.SMEM), pl.BlockSpec(memory_space=pltpu.VMEM)
    hbm = pl.BlockSpec(memory_space=pl.ANY)
    sizes = tuple(len(group) for group in groups)
    pieces = [half for group in groups for piece in group for half in piece]
    count = sum(piece.shape[0] for piece in pieces) // 2

    def body(*refs):
        pair_kernel(*refs, sizes=sizes, final=final)

    return pl.pallas_call(
        body,
        in_specs=[smem, hbm, hbm, vmem, vmem] + [hbm] * len(pieces),
        out_specs=hbm,
        out_shape=jax.ShapeDtypeStruct((512, 2048), jnp.float32),
        scratch_shapes=[
            pltpu.VMEM((512, 2048), jnp.bfloat16),
            pltpu.VMEM((count, 2048), jnp.bfloat16),
            pltpu.VMEM((512, 2048), jnp.float32),
            pltpu.VMEM((512, 2048), jnp.float32),
            pltpu.SemaphoreType.DMA((len(pieces),)),
            pltpu.SemaphoreType.DMA((18,)),
        ],
        name="pair_last" if final else "pair",
    )(table, own, total, row, col, *pieces)


def on_chip(value):
    return pltpu.with_memory_space_constraint(value, pltpu.VMEM)


def energies(me, owner_table, pair_order, occ_energy, vir_energy):
    occ_idx, vir_idx = me // 8, me % 8
    one_hot = (owner_table[:, None] == jnp.arange(128, dtype=jnp.int32)[None, :]).astype(jnp.float32)
    eps = jnp.dot(one_hot, occ_energy, precision=lax.Precision.HIGHEST)
    own_eps = lax.dynamic_slice_in_dim(eps, occ_idx * 8, 8, 0)
    block_eps = lax.dynamic_slice_in_dim(vir_energy, vir_idx * 64, 64, 0)
    row = (own_eps[:, None] - block_eps[None, :]).reshape(512, 1)
    row = jnp.broadcast_to(row, (512, 128))
    partner_eps = jnp.concatenate(
        [lax.dynamic_slice_in_dim(eps, pair_order[s] * 8 + vir_idx, 1, 0) for s in range(4)]
    )
    mine = (occ_idx // 4 + occ_idx // 2 % 2 * 2) % 4
    virtuals = jnp.concatenate([vir_energy, vir_energy]).reshape(8, 128)
    virtuals = lax.dynamic_slice_in_dim(virtuals, mine, 4, 0)
    near = partner_eps[:, None] - virtuals[:1]
    beside = partner_eps[None, :, None] - jnp.stack([virtuals[3], virtuals[1]])[:, None, :]
    across = partner_eps[:, None] - virtuals[2:3]
    first = beside[:, :2].reshape(1, 512)
    second = jnp.concatenate([beside[:, 2:].reshape(1, 512), across.reshape(1, 512)], axis=1)
    return row, near.reshape(1, 512), first, second


def whole(three_index, virt_coeff, metric_root, owner_table, pair_order, occ_energy, vir_energy):
    me = lax.axis_index("occ") * 8 + lax.axis_index("vir")
    mine_parts, other_parts = gathered_metric(metric_root)
    part, own = transformed(pair_order, owner_table, three_index, virt_coeff)
    part = lax.all_to_all(part, AXES, split_axis=0, concat_axis=0, tiled=True)
    own = lax.all_to_all(own, AXES, split_axis=0, concat_axis=0, tiled=True)
    part, own = part.reshape(2048, 256), own.reshape(2048, 512)

    energy = energies(me, owner_table, pair_order, occ_energy, vir_energy)
    table = lax.dynamic_slice_in_dim(jnp.asarray(metric_table()), me, 1, 0).reshape(129)
    part, table, *energy = lax.optimization_barrier((part, table, *energy))
    row, near, first, second = energy
    other = swapped(part)
    here, *halves = partner_fit(table, part, other, mine_parts)

    def whole_rows(part):
        return part, swapped(part)

    beside = []
    for half in range(2):
        beside.append([shifted(halves[half], ("y", "y"), by) for by in (1, 3)])
    across = shifted(here, ("z", "z"), 2)
    here = whole_rows(here)
    beside = [[whole_rows(part) for part in beside[i]] for i in range(2)]
    across = whole_rows(across)
    across = tuple(on_chip(half) for half in across)
    own, density = own_and_pair(table, own, row, near, mine_parts + other_parts, [[here]])
    density = paired(table, own, density, row, first, [beside[0]], False)
    density = paired(table, own, density, row, second, [beside[1], [across]], True)
    return density.reshape(8, 64, 2048)


def solution(mesh):
    placed = (P(AXES, None, None), P(), P(AXES, None), P(), P(), P(), P())
    return jax.shard_map(
        whole, mesh=mesh, in_specs=placed, out_specs=P("occ", "vir", None), check_vma=False
    )
```

```python
import numpy as np
import jax
import jax.numpy as jnp
from jax import lax
from jax.experimental import pallas as pl
from jax.experimental.pallas import tpu as pltpu
from jax.sharding import PartitionSpec as P


AXES = ("occ", "vir")
SIZE = {"x": 4, "y": 4, "z": 4}
ORDER = (("z", "x", "y"), ("y", "z", "x"))


def line(p):
    return ((p["y"] * 2 + p["z"] // 2) * 2 + p["c"]) * 8 + p["x"] * 2 + p["z"] % 2


def places():
    return [
        dict(x=x, y=y, z=z, c=c)
        for x in range(4)
        for y in range(4)
        for z in range(4)
        for c in range(2)
    ]


def moved(p, dim, by):
    q = dict(p)
    q[dim] = (q[dim] + by) % SIZE[dim]
    return q


def shifted(value, dims, by):
    pairs = [(line(p), line(moved(p, dims[p["c"]], by))) for p in places()]
    return lax.ppermute(value, AXES, pairs)


def swapped(value):
    pairs = [(line(p), line(dict(p, c=1 - p["c"]))) for p in places()]
    return lax.ppermute(value, AXES, pairs)


def metric_table():
    table = np.zeros((128, 129), np.int32)
    for p in places():
        for buf in range(8):
            core = p["c"] if buf < 4 else 1 - p["c"]
            first, second, third = ORDER[core]
            for k2 in range(4):
                for k1 in range(4):
                    q = dict(p, c=core)
                    for dim, by in ((third, buf % 4), (second, k2), (first, k1)):
                        q = moved(q, dim, -by)
                    block = line(q) // 16 * 8 + line(q) % 8 + (buf // 4) * 64
                    table[line(p), buf * 16 + k2 * 4 + k1] = block
        table[line(p), 128] = p["c"]
    return table


def gathered_metric(rows):
    for stage in (0, 1):
        dims = (ORDER[0][stage], ORDER[1][stage])
        got = [shifted(rows, dims, by) for by in (1, 2, 3)]
        rows = jnp.concatenate([rows] + got, axis=0)
    dims = (ORDER[0][2], ORDER[1][2])
    mine = [rows] + [shifted(rows, dims, by) for by in (1, 2, 3)]
    return mine, [swapped(part) for part in mine]


PITCH = 168


def half_kernel(order_ref, owner_ref, ints_ref, coeff_ref, part_ref, own_ref, *scratches):
    ints, scratch, pick_ref, part, own, in_sems, out_sems = scratches
    takes = [
        pltpu.make_async_copy(
            ints_ref.at[pl.ds(c * 4, 4)], ints.at[pl.ds(c * 4, 4)], in_sems.at[c]
        )
        for c in range(4)
    ]
    for take in takes:
        take.start()
    owners = jnp.broadcast_to(owner_ref[...].astype(jnp.float32), (128, 128)).T
    orbital = lax.broadcasted_iota(jnp.int32, (128, 128), 1).astype(jnp.float32)
    pick_ref[0:128, :] = jnp.where(owners == orbital, 1.0, 0.0)
    for s in range(4):
        first = pl.multiple_of(order_ref[s] * 8, 8)
        pick_ref[128 + 8 * s:136 + 8 * s, :] = pick_ref[pl.ds(first, 8), :]
    pick = pick_ref[...].astype(jnp.bfloat16)

    for c in range(4):
        takes[c].wait()
        half = jnp.dot(
            ints[c * 4:c * 4 + 4].reshape(512, 640),
            coeff_ref[...],
            preferred_element_type=jnp.float32,
        ).astype(jnp.bfloat16)
        for i in range(4):
            rows = jnp.dot(
                pick, half[i * 128:i * 128 + 128], preferred_element_type=jnp.float32
            )
            at = (c * 4 + i) * PITCH
            for t in range(4):
                scratch[t, at:at + 160, :] = rows[:, t * 128:t * 128 + 128]

    lane = lax.broadcasted_iota(jnp.int32, (16, 128), 1)
    low = lane < 64

    def rows_of(t, position):
        return scratch.at[t][pl.ds(position, 16, stride=PITCH), :]

    def emit_partner(v, carry):
        for t in range(4):
            for s in range(4):
                tile = rows_of(t, 128 + s * 8 + v).astype(part.dtype)
                at = slice(s % 2 * 128, s % 2 * 128 + 128)
                for z in range(2):
                    owner = ((t + 2 * z) % 4 * 2 + z) * 2 + s // 2
                    part[owner * 8 + v, :, at] = tile
        return carry

    lax.fori_loop(0, 8, emit_partner, 0, unroll=2)
    send_part = pltpu.make_async_copy(part, part_ref, out_sems.at[0])
    send_part.start()

    def emit(group, carry):
        to = pl.multiple_of(group * 8, 8)
        for t in range(4):
            for j in range(4):
                even = rows_of(t, group * 8 + 2 * j)
                odd = rows_of(t, group * 8 + 2 * j + 1)
                first = jnp.where(low, even, pltpu.roll(odd, 64, 1))
                second = jnp.where(low, pltpu.roll(even, 64, 1), odd)
                at = slice(j * 128, j * 128 + 128)
                own[to + 2 * t, :, at] = first.astype(own.dtype)
                own[to + 2 * t + 1, :, at] = second.astype(own.dtype)
        return carry

    sends = [
        pltpu.make_async_copy(
            own.at[pl.ds(h * 64, 64)], own_ref.at[pl.ds(h * 64, 64)], out_sems.at[1 + h]
        )
        for h in range(2)
    ]
    for h in range(2):
        lax.fori_loop(8 * h, 8 * h + 8, emit, 0, unroll=4)
        sends[h].start()
    send_part.wait()
    for send in sends:
        send.wait()


def transformed(pair_order, owner_table, three_index, virt_coeff):
    vmem, hbm = pl.BlockSpec(memory_space=pltpu.VMEM), pl.BlockSpec(memory_space=pl.ANY)
    part = jax.ShapeDtypeStruct((128, 16, 256), jnp.bfloat16)
    own = jax.ShapeDtypeStruct((128, 16, 512), jnp.bfloat16)
    return pl.pallas_call(
        half_kernel,
        in_specs=[pl.BlockSpec(memory_space=pltpu.SMEM), vmem, hbm, vmem],
        out_specs=[hbm, hbm],
        out_shape=[part, own],
        scratch_shapes=[
            pltpu.VMEM((16, 128, 640), jnp.bfloat16),
            pltpu.VMEM((4, 16 * PITCH, 128), jnp.float32),
            pltpu.VMEM((160, 128), jnp.float32),
            pltpu.VMEM(part.shape, part.dtype),
            pltpu.VMEM(own.shape, own.dtype),
            pltpu.SemaphoreType.DMA((4,)),
            pltpu.SemaphoreType.DMA((3,)),
        ],
        name="half",
    )(pair_order, owner_table.reshape(1, 128), three_index, virt_coeff)


def place(table_ref, parts, first, metric, sems):
    for i, part in enumerate(parts):

        def start(j, carry, i=i, part=part):
            row = pl.multiple_of(table_ref[(first + i) * 16 + j] * 16, 16)
            pltpu.make_async_copy(
                part.at[pl.ds(pl.multiple_of(j * 16, 16), 16)],
                metric.at[pl.ds(row, 16)],
                sems.at[first + i],
            ).start()
            return carry

        lax.fori_loop(0, 16, start, 0)


def placed(parts, first, metric, sems):
    for i, part in enumerate(parts):
        pltpu.make_async_copy(part, metric.at[pl.ds(0, 256)], sems.at[first + i]).wait()


def fitted(left, metric):
    return lax.dot_general(
        left, metric, (((1,), (1,)), ((), ())), preferred_element_type=jnp.float32
    ).astype(jnp.bfloat16)


def partner_kernel(table_ref, mine_ref, other_ref, *refs):
    parts, outs, (rows, metric, sems, row_sems) = refs[:4], refs[4:7], refs[7:]
    core = table_ref[128]
    takes = [
        pltpu.make_async_copy(mine_ref, rows.at[core], row_sems.at[0]),
        pltpu.make_async_copy(other_ref, rows.at[1 - core], row_sems.at[1]),
    ]
    for take in takes:
        take.start()
    place(table_ref, parts, 0, metric, sems)
    for take in takes:
        take.wait()
    left = jnp.concatenate([rows[c].T for c in range(2)], axis=0)
    placed(parts, 0, metric, sems)
    for block in range(2):
        at = slice(block * 512, block * 512 + 512)
        got = fitted(left, metric[at, :])
        outs[0][:, at] = got
        outs[1][:, at] = got[:256]
        outs[2][:, at] = got[256:]


def partner_fit(table, mine, other, parts):
    smem, vmem = pl.BlockSpec(memory_space=pltpu.SMEM), pl.BlockSpec(memory_space=pltpu.VMEM)
    return pl.pallas_call(
        partner_kernel,
        in_specs=[smem] + [pl.BlockSpec(memory_space=pl.ANY)] * 6,
        out_specs=[vmem] * 3,
        out_shape=[jax.ShapeDtypeStruct((rows, 1024), jnp.bfloat16) for rows in (512, 256, 256)],
        scratch_shapes=[
            pltpu.VMEM((2, 2048, 256), jnp.bfloat16),
            pltpu.VMEM((1024, 2048), jnp.bfloat16),
            pltpu.SemaphoreType.DMA((4,)),
            pltpu.SemaphoreType.DMA((2,)),
        ],
        name="fit_partner",
    )(table, mine, other, *parts)


def fetch(groups, buf, sems):
    found, at, used = [], 0, 0
    for group in groups:
        start, copies = at, []
        for piece in group:
            rows = piece[0].shape[0]
            for half in range(2):
                to = buf.at[pl.ds(at, rows), pl.ds(half * 1024, 1024)]
                copies.append(pltpu.make_async_copy(piece[half], to, sems.at[used]))
                used += 1
            at += rows
        for copy in copies:
            copy.start()
        found.append((start, at, copies))
    return found


def contribute(own, part, row, col, total, fresh, carried, finished):
    pair = lax.dot_general(
        own[...], part, (((1,), (1,)), ((), ())), preferred_element_type=jnp.float32
    )
    amp = (pair / (row + col)).astype(jnp.bfloat16)
    if carried is not None:
        carried[1].wait()
    for chunk in range(4):
        at = slice(chunk * 512, chunk * 512 + 512)
        term = jnp.dot(amp, part[:, at], preferred_element_type=jnp.float32)
        if not fresh:
            term = total[:, at] + term
        if carried is not None:
            term = carried[0][:, at] + term
        total[:, at] = term
        finished(chunk)


def grouped(refs, sizes):
    groups, at = [], 0
    for size in sizes:
        groups.append([refs[at + 2 * i:at + 2 * i + 2] for i in range(size)])
        at += 2 * size
    return groups


def own_kernel(table_ref, rows_ref, row_ref, col_ref, *refs, sizes):
    count = 2 * sum(sizes)
    parts, pieces, refs = refs[:8], refs[8:8 + count], refs[8 + count:]
    own_ref, total_ref, metric, own, buf, total, sems, piece_sems, more = refs
    place(table_ref, parts, 0, metric, sems)
    groups = fetch(grouped(pieces, sizes), buf, piece_sems)
    left = rows_ref[...].T
    for half in range(2):
        placed(parts[half * 4:half * 4 + 4], half * 4, metric, sems)
        for block in range(2):
            first = half * 1024 + block * 512
            at = slice(first, first + 512)
            own[:, at] = fitted(left, metric[at, :])
    sends = [pltpu.make_async_copy(own, own_ref, more.at[1])]
    sends[0].start()
    row = row_ref[:, :1]
    for index, (start, stop, copies) in enumerate(groups):
        for copy in copies:
            copy.wait()

        def finished(chunk, last=index == len(groups) - 1):
            if last:
                at = pl.ds(chunk * 512, 512)
                sends.append(
                    pltpu.make_async_copy(total.at[:, at], total_ref.at[:, at], more.at[2 + chunk])
                )
                sends[-1].start()

        contribute(
            own, buf[start:stop, :], row, col_ref[:, start:stop], total,
            index == 0, None, finished,
        )
    for send in sends:
        send.wait()


def own_and_pair(table, own, row, col, parts, groups):
    smem, vmem = pl.BlockSpec(memory_space=pltpu.SMEM), pl.BlockSpec(memory_space=pltpu.VMEM)
    hbm = pl.BlockSpec(memory_space=pl.ANY)
    sizes = tuple(len(group) for group in groups)
    pieces = [half for group in groups for piece in group for half in piece]
    count = sum(piece.shape[0] for piece in pieces) // 2

    def body(*refs):
        own_kernel(*refs, sizes=sizes)

    return pl.pallas_call(
        body,
        in_specs=[smem, vmem, vmem, vmem] + [hbm] * (8 + len(pieces)),
        out_specs=[hbm] * 2,
        out_shape=[
            jax.ShapeDtypeStruct((512, 2048), jnp.bfloat16),
            jax.ShapeDtypeStruct((512, 2048), jnp.float32),
        ],
        scratch_shapes=[
            pltpu.VMEM((2048, 2048), jnp.bfloat16),
            pltpu.VMEM((512, 2048), jnp.bfloat16),
            pltpu.VMEM((count, 2048), jnp.bfloat16),
            pltpu.VMEM((512, 2048), jnp.float32),
            pltpu.SemaphoreType.DMA((8,)),
            pltpu.SemaphoreType.DMA((len(pieces),)),
            pltpu.SemaphoreType.DMA((6,)),
        ],
        name="own_and_pair",
    )(table, on_chip(own), row, col, *parts, *pieces)


def pair_kernel(table_ref, own_ref, total_ref, row_ref, col_ref, *refs, sizes, final):
    count = 2 * sum(sizes)
    pieces, (out_ref, own, buf, before, total, piece_sems, more) = refs[:count], refs[count:]
    core = table_ref[128]
    take = pltpu.make_async_copy(own_ref, own, more.at[0])
    take.start()
    groups = fetch(grouped(pieces, sizes), buf, piece_sems)
    carried = pltpu.make_async_copy(total_ref, before, more.at[1])
    carried.start()
    row = row_ref[:, :1]
    take.wait()
    sends = []

    for index, (start, stop, copies) in enumerate(groups):
        for copy in copies:
            copy.wait()

        def finished(chunk, last=index == len(groups) - 1):
            if last:
                for tile in range(chunk * 4, chunk * 4 + 4):
                    to = tile * 128
                    if final:
                        half = core if tile < 8 else 1 - core
                        to = pl.multiple_of(((tile % 8) * 2 + half) * 128, 128)
                    sends.append(
                        pltpu.make_async_copy(
                            total.at[:, pl.ds(tile * 128, 128)],
                            out_ref.at[:, pl.ds(to, 128)],
                            more.at[2 + tile],
                        )
                    )
                    sends[-1].start()

        contribute(
            own, buf[start:stop, :], row, col_ref[:, start:stop], total,
            index == 0, (before, carried) if index == len(groups) - 1 else None, finished,
        )
    for send in sends:
        send.wait()


def paired(table, own, total, row, col, groups, final):
    smem, vmem = pl.BlockSpec(memory_space=pltpu.SMEM), pl.BlockSpec(memory_space=pltpu.VMEM)
    hbm = pl.BlockSpec(memory_space=pl.ANY)
    sizes = tuple(len(group) for group in groups)
    pieces = [half for group in groups for piece in group for half in piece]
    count = sum(piece.shape[0] for piece in pieces) // 2

    def body(*refs):
        pair_kernel(*refs, sizes=sizes, final=final)

    return pl.pallas_call(
        body,
        in_specs=[smem, hbm, hbm, vmem, vmem] + [hbm] * len(pieces),
        out_specs=hbm,
        out_shape=jax.ShapeDtypeStruct((512, 2048), jnp.float32),
        scratch_shapes=[
            pltpu.VMEM((512, 2048), jnp.bfloat16),
            pltpu.VMEM((count, 2048), jnp.bfloat16),
            pltpu.VMEM((512, 2048), jnp.float32),
            pltpu.VMEM((512, 2048), jnp.float32),
            pltpu.SemaphoreType.DMA((len(pieces),)),
            pltpu.SemaphoreType.DMA((18,)),
        ],
        name="pair_last" if final else "pair",
    )(table, own, total, row, col, *pieces)


def on_chip(value):
    return pltpu.with_memory_space_constraint(value, pltpu.VMEM)


def energies(me, owner_table, pair_order, occ_energy, vir_energy):
    occ_idx, vir_idx = me // 8, me % 8
    one_hot = (owner_table[:, None] == jnp.arange(128, dtype=jnp.int32)[None, :]).astype(jnp.float32)
    eps = jnp.dot(one_hot, occ_energy, precision=lax.Precision.HIGHEST)
    own_eps = lax.dynamic_slice_in_dim(eps, occ_idx * 8, 8, 0)
    block_eps = lax.dynamic_slice_in_dim(vir_energy, vir_idx * 64, 64, 0)
    row = (own_eps[:, None] - block_eps[None, :]).reshape(512, 1)
    row = jnp.broadcast_to(row, (512, 128))
    partner_eps = jnp.concatenate(
        [lax.dynamic_slice_in_dim(eps, pair_order[s] * 8 + vir_idx, 1, 0) for s in range(4)]
    )
    mine = (occ_idx // 4 + occ_idx // 2 % 2 * 2) % 4
    virtuals = jnp.concatenate([vir_energy, vir_energy]).reshape(8, 128)
    virtuals = lax.dynamic_slice_in_dim(virtuals, mine, 4, 0)
    near = partner_eps[:, None] - virtuals[:1]
    beside = partner_eps[None, :, None] - jnp.stack([virtuals[3], virtuals[1]])[:, None, :]
    across = partner_eps[:, None] - virtuals[2:3]
    first = beside[:, :2].reshape(1, 512)
    second = jnp.concatenate([across.reshape(1, 512), beside[:, 2:].reshape(1, 512)], axis=1)
    return row, near.reshape(1, 512), first, second


def whole(three_index, virt_coeff, metric_root, owner_table, pair_order, occ_energy, vir_energy):
    me = lax.axis_index("occ") * 8 + lax.axis_index("vir")
    mine_parts, other_parts = gathered_metric(metric_root)
    part, own = transformed(pair_order, owner_table, three_index, virt_coeff)
    part = lax.all_to_all(part, AXES, split_axis=0, concat_axis=0, tiled=True)
    own = lax.all_to_all(own, AXES, split_axis=0, concat_axis=0, tiled=True)
    part, own = part.reshape(2048, 256), own.reshape(2048, 512)

    energy = energies(me, owner_table, pair_order, occ_energy, vir_energy)
    table = lax.dynamic_slice_in_dim(jnp.asarray(metric_table()), me, 1, 0).reshape(129)
    part, table, *energy = lax.optimization_barrier((part, table, *energy))
    row, near, first, second = energy
    other = swapped(part)
    here, *halves = partner_fit(table, on_chip(part), other, mine_parts)

    def whole_rows(part):
        return part, swapped(part)

    beside = []
    for half in range(2):
        beside.append([shifted(halves[half], ("y", "y"), by) for by in (1, 3)])
    across = shifted(here, ("z", "z"), 2)
    here = whole_rows(here)
    beside = [[whole_rows(part) for part in beside[i]] for i in range(2)]
    across = whole_rows(across)
    across = tuple(on_chip(half) for half in across)
    own, density = own_and_pair(table, own, row, near, mine_parts + other_parts, [[here]])
    density = paired(table, own, density, row, first, [beside[0]], False)
    density = paired(table, own, density, row, second, [[across], beside[1]], True)
    return density.reshape(8, 64, 2048)


def solution(mesh):
    placed = (P(AXES, None, None), P(), P(AXES, None), P(), P(), P(), P())
    return jax.shard_map(
        whole, mesh=mesh, in_specs=placed, out_specs=P("occ", "vir", None), check_vma=False
    )
```
